32 devices in a mesh: ctx: 8 (over z, core), exp: 4 (over y, x).
Axes of the slice: x: 2, y: 2, z: 4, core: 2. Of those that a mesh axis runs over, the one named last changes fastest.
Arguments:
- queries: bfloat16 [4, 1024, 8192], P('exp', 'ctx'), may hold values from -64 to 64
- key_head_vectors: bfloat16 [4, 1024, 512], P('exp', 'ctx'), may hold values from -6 to 6
- value_head_vectors: bfloat16 [4, 1024, 512], P('exp', 'ctx'), may hold values from -6 to 6
- segment_ids: int32 [4, 1024], P('exp', 'ctx'), may hold values from 0 to 3, never falling along the last dimension, each value on 1 to 512 neighbouring positions
- normed: bfloat16 [4, 1024, 4096], P('exp', 'ctx'), may hold values from -6 to 6
- expert_ids: int32 [4, 1024, 2], P('exp', 'ctx'), may hold values from 0 to 3, all different within a row; in each aligned block of 128 rows (0 to 127, 128 to 255, ..., all dimensions but the last counted through in order) at most 80 rows name the same one
- gate_probs: float32 [4, 1024, 2], P('exp', 'ctx'), may hold values from 0.1 to 1
- gate_weight: bfloat16 [4, 768, 4096], P('exp', 'ctx'), may hold values from -0.09375 to 0.09375
- up_weight: bfloat16 [4, 768, 4096], P('exp', 'ctx'), may hold values from -0.09375 to 0.09375
- down_weight: bfloat16 [4, 768, 4096], P('exp', 'ctx'), may hold values from -0.21875 to 0.21875
Outputs:
- context: bfloat16 [4, 1024, 8192], P('exp', 'ctx')
- expert_mix: bfloat16 [4, 1024, 4096], P('exp', 'ctx')
The draws below stay inside these ranges and needn't reach their ends.
Inputs may be any that keep to these rules, and one draw needn't show every extreme that they name: `segment_ids`: ids never fall along a sequence; an even id marks a document, an odd id the question that reads the document just before it; each segment holds at most 512 positions and one holds exactly that many. `expert_ids`: each position names 2 different experts. Within the rows of one device no expert is named more than 80 times, a bound that some block reaches.
All inputs are finite; a program needn't handle non-finite values.
Results may differ from the reference program's by a relative error of at most 0.0058.
Values may be sent and summed in bfloat16 or wider, within the bound.
A program may use at most 128 MiB of HBM per device.

```python
import math
import jax
import jax.numpy as jnp
import numpy as np
from jax import lax

D = 4096
QUERY_HEAD_COUNT = 64
KEY_HEAD_COUNT = 4
HEAD_SIZE = 128
FF = 768
TOPK = 2
TOK_DEV = 128
EXPERTS = 4
SEQUENCE_LENGTH = 1024
SEQUENCE_COUNT = 4
CAP = 80
N_CTX = 8


def draw_pairs(key):
    start_offset = jax.random.fold_in(key, 7)
    query_result = jnp.clip(jax.random.normal(jax.random.fold_in(start_offset, 1), (SEQUENCE_COUNT, SEQUENCE_LENGTH, QUERY_HEAD_COUNT, HEAD_SIZE), jnp.float32), -6.0, 6.0)
    key_result = jnp.clip(jax.random.normal(jax.random.fold_in(start_offset, 2), (SEQUENCE_COUNT, SEQUENCE_LENGTH, KEY_HEAD_COUNT, HEAD_SIZE), jnp.float32), -6.0, 6.0)
    return (query_result.reshape(SEQUENCE_COUNT, SEQUENCE_LENGTH, QUERY_HEAD_COUNT * HEAD_SIZE), key_result.reshape(SEQUENCE_COUNT, SEQUENCE_LENGTH, KEY_HEAD_COUNT * HEAD_SIZE))


def draw_queries(key, part):
    return draw_pairs(key)[0].astype(jnp.bfloat16)


def draw_key_head_vectors(key, part):
    return draw_pairs(key)[1].astype(jnp.bfloat16)


def level_of(key, dims, pieces, smallest, top_value):
    level, own = 1.0, jax.random.fold_in(key, 6)
    for axis_at, blocks in pieces:
        steps = jnp.exp(jax.random.uniform(jax.random.fold_in(own, axis_at), (blocks,), jnp.float32, smallest / len(pieces), top_value / len(pieces)))
        level = level * jnp.repeat(steps, dims[axis_at] // blocks).reshape([-1 if axis == axis_at else 1 for axis in range(len(dims))])
    return level


def length_profile(count, total, most, skew):
    weights = [(1 << 20) // math.isqrt(standing ** skew) + 1 for standing in range(2, count + 1)]
    spare, holding = total - most - (count - 1), [1] * (count - 1)
    while spare > 0:
        movable = [i for i in range(count - 1) if holding[i] < most]
        mass, remaining = sum([weights[i] for i in movable]), spare
        for i in movable:
            more = min(most - holding[i], max(1, remaining * weights[i] // mass), spare)
            holding[i] = holding[i] + more
            spare = spare - more
    return np.array([most] + holding)


def ragged_sizes(key, number_of, total, most, skew):
    if number_of == 2:
        one = jax.random.randint(key, (), max(1, total - most), min(most, total - 1) + 1)
        return jnp.stack([one, total - one])
    tallies = jnp.asarray(length_profile(number_of, total, most, skew), jnp.int32)
    twos = (number_of - 1) // 2
    donor, receiver = tallies[1:1 + 2 * twos:2], tallies[2:2 + 2 * twos:2]
    room = jnp.minimum(donor - 1, most - receiver)
    moved = jax.random.randint(jax.random.fold_in(key, 1), (twos,), 0, 1 << 20) % (room + 1)
    tallies = tallies.at[1:1 + 2 * twos:2].set(donor - moved).at[2:2 + 2 * twos:2].set(receiver + moved)
    return tallies[jax.random.permutation(jax.random.fold_in(key, 2), number_of)]


def deal_out(stream_key, own, number, rows, count, top, limit, skew):
    order = jax.random.permutation(stream_key, count)
    crowded, ordinary = load_shares(count, rows * top, limit, skew, True), load_shares(count, rows * top, limit, skew, False)
    places = jnp.arange(count)

    def named(lengths, rotation):
        used = int((lengths > 0).sum())
        fixed = max(1, used // 4)
        shifted = fixed + (places - fixed + rotation * (used - fixed)) % max(1, count - fixed)
        return jnp.zeros((count,), jnp.int32).at[order[jnp.where(places < fixed, places, shifted)]].set(jnp.asarray(lengths, jnp.int32))

    lengths = jnp.where(number % 4 == 0, named(crowded, number // 4), named(ordinary, number - number // 4 - 1))
    mixed = jax.random.permutation(jax.random.fold_in(own, 3), count)
    source_of, sink = mixed[0:count // 2 * 2:2], mixed[1:count // 2 * 2:2]
    room = jnp.minimum(lengths[source_of] - 1, limit - lengths[sink]) // 2
    room = jnp.where((source_of == order[0]) | (sink == order[0]) | (lengths[sink] == 0), 0, jnp.maximum(room, 0))
    shifted = jax.random.randint(jax.random.fold_in(own, 4), (count // 2,), 0, 1 << 20) % (room + 1)
    lengths = lengths.at[source_of].add(-shifted).at[sink].add(shifted)
    items = jnp.searchsorted(jnp.cumsum(lengths), jnp.arange(rows * top), side="right").astype(jnp.int32)
    table = items.reshape(top, rows).T
    table = table[jax.random.permutation(jax.random.fold_in(own, 1), rows)]
    rotation = jax.random.randint(jax.random.fold_in(own, 2), (rows, 1), 0, top)
    return jnp.take_along_axis(table, (jnp.arange(top)[None, :] + rotation) % top, axis=1)


def load_shares(number_of, total, reach, skew, full):
    loads = [(1 << 20) // math.isqrt(standing ** skew) + 1 for standing in range(1, number_of + 1)]
    largest = reach if full else min(reach, max(-(-total // number_of), total * loads[0] // sum(loads)))
    least = 1 if total - largest >= number_of - 1 else 0
    given, spare = [largest] + [least] * (number_of - 1), total - largest - least * (number_of - 1)
    while spare > 0:
        free = [i for i in range(1, number_of) if given[i] < largest] or [i for i in range(1, number_of) if given[i] < reach]
        mass, left = sum([loads[i] for i in free]), spare
        for i in free:
            extra = min(reach - given[i], max(1, left * loads[i] // mass), spare)
            given[i] = given[i] + extra
            spare = spare - extra
    return np.array(given)


def scatter_about(key, extent, scale, reach, cuts=(), held_as=jnp.bfloat16):
    drawn = scale * jax.random.normal(key, extent, jnp.float32)
    if cuts:
        drawn = drawn * level_of(key, extent, cuts, -0.22, 0.18)
    return jnp.clip(drawn, -reach, reach).astype(held_as)


def setup_inputs(seed: int = 0) -> dict:
    key_list = jax.random.split(jax.random.key(seed), 11)
    queries = draw_queries(jax.random.fold_in(key_list[10], 71), 0)
    key_head_vectors = draw_key_head_vectors(jax.random.fold_in(key_list[10], 71), 0)
    value_head_vectors = scatter_about(key_list[2], (SEQUENCE_COUNT, SEQUENCE_LENGTH, KEY_HEAD_COUNT * HEAD_SIZE), 1.0, 6.0, ((0, 4), (1, 8)))
    segment_ids = jax.vmap(lambda own: jnp.searchsorted(jnp.cumsum(ragged_sizes(own, 4, SEQUENCE_LENGTH, SEQUENCE_LENGTH // 2, 1)), jnp.arange(SEQUENCE_LENGTH), side="right"))(jax.random.split(key_list[3], SEQUENCE_COUNT)).reshape((SEQUENCE_COUNT, SEQUENCE_LENGTH)).astype(jnp.int32)
    normed = scatter_about(key_list[4], (SEQUENCE_COUNT, SEQUENCE_LENGTH, D), 1.0, 6.0, ((0, 4), (1, 8)))
    expert_ids_keys = jax.random.split(jax.random.fold_in(key_list[5], 1), SEQUENCE_COUNT * SEQUENCE_LENGTH // TOK_DEV)
    expert_ids_turns = jax.random.permutation(jax.random.fold_in(key_list[5], 3), SEQUENCE_COUNT * SEQUENCE_LENGTH // TOK_DEV)
    expert_ids = jax.vmap(lambda own, number: deal_out(jax.random.fold_in(key_list[5], 2), own, number, TOK_DEV, EXPERTS, TOPK, CAP, 2))(expert_ids_keys, expert_ids_turns).reshape((SEQUENCE_COUNT, SEQUENCE_LENGTH, TOPK))
    gate_probs = jnp.clip(0.1 + 0.9 * jax.random.uniform(key_list[6], (SEQUENCE_COUNT, SEQUENCE_LENGTH, TOPK), jnp.float32) ** level_of(key_list[6], (SEQUENCE_COUNT, SEQUENCE_LENGTH, TOPK), ((0, 4), (1, 8)), -0.2, 0.2), 0.1, 1.0)
    gate_weight = scatter_about(key_list[7], (EXPERTS, FF, D), D ** -0.5, 0.09375, ((0, 4), (1, 8)))
    up_weight = scatter_about(key_list[8], (EXPERTS, FF, D), D ** -0.5, 0.09375, ((0, 4), (1, 8)))
    down_weight = scatter_about(key_list[9], (EXPERTS, FF, D), FF ** -0.5, 0.21875, ((0, 4), (1, 8)))
    return dict(queries=queries, key_head_vectors=key_head_vectors, value_head_vectors=value_head_vectors, segment_ids=segment_ids, normed=normed, expert_ids=expert_ids, gate_probs=gate_probs, gate_weight=gate_weight, up_weight=up_weight, down_weight=down_weight)


def attend_mask(query_places, key_places, query_segments, key_segments):
    causal = key_places[None, :] <= query_places[:, None]
    same_segment = key_segments[None, :] == query_segments[:, None]
    source = (query_segments[:, None] % 2 == 1) & (key_segments[None, :] == query_segments[:, None] - 1)
    return causal & (same_segment | source)


def attend_sequence(operands):
    queries, key_head_vectors, value_head_vectors, segment_ids = operands
    span_length = queries.shape[0]
    query_group_count = QUERY_HEAD_COUNT // KEY_HEAD_COUNT
    query_head_rows = queries.astype(jnp.float32).reshape(span_length, KEY_HEAD_COUNT, query_group_count, HEAD_SIZE).transpose(1, 2, 0, 3)
    key_head_rows = key_head_vectors.astype(jnp.float32).reshape(span_length, KEY_HEAD_COUNT, HEAD_SIZE).transpose(1, 0, 2)
    value_head_rows = value_head_vectors.astype(jnp.float32).reshape(span_length, KEY_HEAD_COUNT, HEAD_SIZE).transpose(1, 0, 2)
    places = jnp.arange(span_length, dtype=jnp.int32)
    allowed = attend_mask(places, places, segment_ids, segment_ids)

    def per_head(parts):
        query_block, key_block, value_block = parts
        scores = jnp.einsum("gqd,kd->gqk", query_block, key_block) * (HEAD_SIZE ** -0.5)
        masked = jnp.where(allowed[None], scores, -1e30)
        row_peak = jnp.max(masked, axis=-1, keepdims=True)
        exponent = jnp.where(allowed[None], jnp.exp(masked - row_peak), 0.0)
        row_total = jnp.sum(exponent, axis=-1, keepdims=True)
        rounded = lax.optimization_barrier((exponent / row_total).astype(jnp.bfloat16))
        return jnp.einsum("gqk,kd->gqd", rounded.astype(jnp.float32), value_block).astype(jnp.bfloat16)

    heads_out = lax.map(per_head, (query_head_rows, key_head_rows, value_head_rows))
    return heads_out.transpose(2, 0, 1, 3).reshape(span_length, QUERY_HEAD_COUNT * HEAD_SIZE)


def reference(queries, key_head_vectors, value_head_vectors, segment_ids, normed, expert_ids, gate_probs, gate_weight, up_weight, down_weight):
    context = lax.map(attend_sequence, (queries, key_head_vectors, value_head_vectors, segment_ids))
    tokens = normed.reshape(SEQUENCE_COUNT * SEQUENCE_LENGTH, D)
    flat_ids = expert_ids.reshape(SEQUENCE_COUNT * SEQUENCE_LENGTH * TOPK).astype(jnp.int32)
    assigned = SEQUENCE_COUNT * SEQUENCE_LENGTH * TOPK
    owners = jnp.arange(assigned, dtype=jnp.int32) // TOPK
    sorted_order = jnp.argsort(flat_ids, stable=True).astype(jnp.int32)
    expert_range = jnp.arange(EXPERTS, dtype=jnp.int32)
    counts = jnp.sum((flat_ids[None, :] == expert_range[:, None]).astype(jnp.int32), axis=1)
    starts = jnp.sum((flat_ids[None, :] < expert_range[:, None]).astype(jnp.int32), axis=1)
    most_load = SEQUENCE_COUNT * N_CTX * CAP
    padded_order = jnp.concatenate([sorted_order, jnp.zeros((most_load,), jnp.int32)])
    flat_gates = gate_probs.reshape(assigned).astype(jnp.float32)

    def add_expert(running, expert):
        picked_rows = lax.dynamic_slice_in_dim(padded_order, starts[expert], most_load)
        live_slot = jnp.arange(most_load, dtype=jnp.int32) < counts[expert]
        token_rows = owners[picked_rows]
        inputs = tokens[token_rows]
        gate_part = jnp.dot(inputs, gate_weight[expert].T, preferred_element_type=jnp.float32)
        up_part = jnp.dot(inputs, up_weight[expert].T, preferred_element_type=jnp.float32)
        activation = (jax.nn.silu(gate_part) * up_part).astype(jnp.bfloat16)
        result = jnp.dot(activation, down_weight[expert], preferred_element_type=jnp.float32).astype(jnp.bfloat16)
        gate_scale = jnp.where(live_slot, flat_gates[picked_rows], 0.0)
        return running.at[token_rows].add(gate_scale[:, None] * result.astype(jnp.float32)), None

    blended, unused = lax.scan(add_expert, jnp.zeros((SEQUENCE_COUNT * SEQUENCE_LENGTH, D), jnp.float32), expert_range)
    expert_mix = blended.astype(jnp.bfloat16).reshape(SEQUENCE_COUNT, SEQUENCE_LENGTH, D)
    return (context, expert_mix)
```

```python
import functools
import math

import jax
import jax.numpy as jnp
from jax import lax
from jax.experimental import pallas as pl
from jax.experimental.pallas import tpu as pltpu
from jax.sharding import PartitionSpec as P

KEY_HEAD_COUNT = 4
HEAD_SIZE = 128
COLUMN_BLOCKS = 8
HEADS_AT_ONCE = 4
HALVES = 2
WIDE = 2 * HALVES
PIECES = WIDE + COLUMN_BLOCKS
LAG = 2
MESH = pl.DeviceIdType.MESH
F32 = jnp.float32
BF16 = jnp.bfloat16


def kernel(
    n_ctx, n_exp, cap,
    q_hbm, k_hbm, v_hbm, seg_in, x_in, ids_in, prob_in, gate_hbm, up_hbm, down_hbm,
    ctx_out, mix_out,
    q_buf, k_buf, v_buf, seg_buf, bias, weights, x_peer, ids_peer, rows_out, rows_in,
    hidden, hidden_all, result, returned, pick, gates, mix_buf,
    local_sem, kv_send, kv_swap, kv_recv, w_left, w_right, w_swap, w_recv,
    t_send, t_recv, x_send, x_recv, h_send, h_recv, r_send, r_recv, out_sem, mix_sem,
):
    me = lax.axis_index("ctx")
    mine = lax.axis_index("exp")
    n_z = n_ctx // 2
    z, core = me // 2, me % 2
    mate = me + 1 - 2 * core
    peer = z + 1 - 2 * (z % 2)
    hub = jnp.where(z < n_z // 2, z % 2 == 1, z % 2 == 0)
    client = jnp.logical_not(hub)
    inner = (z > 0) & (z < n_z - 1)
    tokens, width = x_in.shape
    group = q_buf.shape[1] // (KEY_HEAD_COUNT * HEAD_SIZE)

    def send(src, dst, send_sem, recv_sem, where):
        return pltpu.make_async_remote_copy(
            src_ref=src, dst_ref=dst, send_sem=send_sem, recv_sem=recv_sem,
            device_id=where, device_id_type=MESH,
        )

    def key_rows(slot):
        return pl.ds(pl.multiple_of(slot * tokens, tokens), tokens)

    own_weights = (gate_hbm, up_hbm, down_hbm)
    columns = width // COLUMN_BLOCKS
    half = width // HALVES

    def block(cb):
        return pl.ds(pl.multiple_of(cb * columns, columns), columns)

    def own_piece(k):
        if isinstance(k, int) and k < WIDE:
            return own_weights[k // HALVES].at[:, pl.ds(k % HALVES * half, half)]
        return down_hbm.at[:, block(k - WIDE)]

    def piece(k, slot):
        if isinstance(k, int) and k < WIDE:
            return weights.at[k // HALVES, slot, :, pl.ds(k % HALVES * half, half)]
        return weights.at[2, slot, :, block(k - WIDE)]

    own_kv = (k_hbm, v_hbm, seg_in)

    def kv_slot(j, slot):
        return seg_buf.at[slot] if j == 2 else (k_buf, v_buf)[j].at[key_rows(slot)]

    def has_side(side):
        return z + 1 < n_z if side else z > 0

    def takes(side):
        return z + 1 < n_z - 1 if side else z > 1

    def peer_side(side):
        return z % 2 == 1 - side

    barrier = pltpu.get_barrier_semaphore()
    for side in (0, 1):
        @pl.when(has_side(side))
        def _():
            pl.semaphore_signal(
                barrier, inc=1, device_id={"ctx": me + 2 if side else me - 2}, device_id_type=MESH
            )
    pl.semaphore_signal(barrier, inc=1, device_id={"ctx": mate}, device_id_type=MESH)
    for d in range(1, n_exp):
        pl.semaphore_signal(barrier, inc=1, device_id={"exp": (mine + d) % n_exp}, device_id_type=MESH)
    pl.semaphore_wait(barrier, n_exp + jnp.where(inner, 2, 1))

    def kv_up(origin, j):
        slot = origin * 2 + core
        src = kv_slot(j, slot)
        return send(src, kv_slot(j, slot), kv_send.at[origin, j], kv_recv.at[slot, j], {"ctx": me + 2})

    def kv_pass(origin, j):
        slot = origin * 2 + core
        src = kv_slot(j, slot)
        return send(src, kv_slot(j, slot), kv_swap.at[origin, j], kv_recv.at[slot, j], {"ctx": mate})

    def kv_own_up(j):
        return send(own_kv[j], kv_slot(j, me), kv_send.at[z, j], kv_recv.at[me, j], {"ctx": me + 2})

    def kv_own_pass(j):
        return send(own_kv[j], kv_slot(j, me), kv_swap.at[z, j], kv_recv.at[me, j], {"ctx": mate})

    @pl.when(has_side(1))
    def _():
        for j in range(3):
            kv_own_up(j).start()
    for j in range(3):
        kv_own_pass(j).start()

    def w_side(side, src, origin, slot, k):
        step = 2 if side else -2
        sem = w_right if side else w_left
        return send(src, piece(k, slot), sem.at[origin, k], w_recv.at[slot, k], {"ctx": me + step})

    def w_mate(src, origin, slot, k):
        return send(src, piece(k, slot), w_swap.at[origin, k], w_recv.at[slot, k], {"ctx": mate})

    def share_wide(k):
        for side in (0, 1):
            @pl.when(takes(side))
            def _():
                w_side(side, own_piece(k), z, me, k).start()

        @pl.when(hub)
        def _():
            w_mate(own_piece(k), z, me, k).start()

    def share_down(side, k):
        w_side(side, own_piece(k), z, me, k).start()

    def each_block(what):
        def one(cb, carry):
            what(cb + WIDE)
            return carry

        lax.fori_loop(0, COLUMN_BLOCKS, one, 0)

    def x_to_hub(j):
        src, dst = ((ids_in, ids_peer), (x_in, x_peer))[j]
        return send(src, dst, t_send.at[j], t_recv.at[j], {"ctx": peer * 2 + core})

    @pl.when(client)
    def _():
        for j in range(2):
            x_to_hub(j).start()
        for k in range(WIDE):
            share_wide(k)

    @pl.when(hub)
    def _():
        share_wide(0)

    for side in (0, 1):
        @pl.when(has_side(side) & (client | peer_side(side)))
        def _():
            each_block(functools.partial(share_down, side))

    each_block(lambda k: w_mate(own_piece(k), z, me, k).start())

    local = [pltpu.make_async_copy(own_weights[k], weights.at[k, me], local_sem.at[k]) for k in range(3)]
    local += [pltpu.make_async_copy(own_kv[j], kv_slot(j, me), local_sem.at[3 + j]) for j in range(3)]
    local += [pltpu.make_async_copy(q_hbm, q_buf, local_sem.at[6])]
    for copy in local:
        copy.start()

    t_row = lax.broadcasted_iota(jnp.int32, (tokens, tokens), 0)
    t_col = lax.broadcasted_iota(jnp.int32, (tokens, tokens), 1)

    def as_column(row):
        return jnp.sum(jnp.where(t_row == t_col, row, jnp.zeros_like(row)), axis=1, keepdims=True)

    def x_out(which, d):
        there = (mine + d) % n_exp
        return send(
            rows_out.at[which, there], rows_in.at[which, mine],
            x_send.at[which, there], x_recv.at[which, mine], {"exp": there},
        )

    def x_arrival(which, d):
        source = (mine + d) % n_exp
        return send(
            rows_out.at[which, source], rows_in.at[which, source],
            x_send.at[which, source], x_recv.at[which, source], {"exp": source},
        )

    def route(which, ids_ref, x_ref):
        ids = ids_ref[...]
        row0, row1 = ids[0:1, :], ids[1:2, :]
        e_row = lax.broadcasted_iota(jnp.int32, (n_exp, tokens), 0)
        named_row = jnp.where((e_row == row0) | (e_row == row1), 1.0, 0.0).astype(F32)
        after = jnp.where(t_row < t_col, 1.0, 0.0).astype(BF16)
        rank_row = jnp.dot(named_row.astype(BF16), after, preferred_element_type=F32)
        place_row = lax.broadcasted_iota(jnp.int32, (cap, tokens), 0).astype(F32)
        x = x_ref[...]
        for e in range(n_exp):
            chosen = jnp.where(place_row == rank_row[e : e + 1, :], named_row[e : e + 1, :], 0.0)
            rows_out[which, e] = jnp.dot(chosen.astype(BF16), x, preferred_element_type=F32).astype(BF16)
        for d in range(1, n_exp):
            x_out(which, d).start()
        rows_in[which, mine] = rows_out[which, mine]

    @pl.when(hub)
    def _():
        route(1, ids_in, x_in)

    def kv_relay(s, carry):
        origin = z - s

        @pl.when(origin >= 0)
        def _():
            for j in range(3):
                kv_pass(origin, j).wait_recv()

                @pl.when(has_side(1))
                def _():
                    kv_up(origin, j).start()

                kv_pass(origin, j).start()

        return carry

    lax.fori_loop(1, n_z, kv_relay, 0)

    @pl.when(hub)
    def _():
        for k in range(1, WIDE):
            share_wide(k)

    ids = ids_in[...]
    probs = prob_in[...]
    id0, id1 = as_column(ids[0:1, :]), as_column(ids[1:2, :])
    e_col = lax.broadcasted_iota(jnp.int32, (tokens, n_exp), 1)
    named_col = jnp.where((e_col == id0) | (e_col == id1), 1.0, 0.0).astype(F32)
    before = jnp.where(t_col < t_row, 1.0, 0.0).astype(BF16)
    rank_col = jnp.dot(before, named_col.astype(BF16), preferred_element_type=F32)
    weight_col = jnp.where(e_col == id0, as_column(probs[0:1, :]), 0.0) + jnp.where(
        e_col == id1, as_column(probs[1:2, :]), 0.0
    )
    place_col = lax.broadcasted_iota(jnp.int32, (tokens, cap), 1).astype(F32)
    for e in range(n_exp):
        back = jnp.where(place_col == rank_col[:, e : e + 1], named_col[:, e : e + 1], 0.0)
        pick[e] = back.astype(BF16)
        gates[e] = weight_col[:, e : e + 1]

    def kv_from_mate(origin, carry):
        slot = origin * 2 + 1 - core

        @pl.when(origin <= z)
        def _():
            for j in range(3):
                send(
                    kv_slot(j, slot), kv_slot(j, slot), kv_swap.at[origin, j], kv_recv.at[slot, j], {"ctx": mate}
                ).wait_recv()

        @pl.when(origin > z)
        def _():
            both = pl.ds(pl.multiple_of(origin * 2 * tokens, 2 * tokens), 2 * tokens)
            k_buf[both] = jnp.zeros((2 * tokens, k_buf.shape[1]), BF16)
            v_buf[both] = jnp.zeros((2 * tokens, v_buf.shape[1]), BF16)
            seg_buf[pl.ds(origin * 2, 2)] = jnp.zeros((2, 1, tokens), jnp.int32)

        return carry

    lax.fori_loop(0, n_z, kv_from_mate, 0)
    for copy in local[3:]:
        copy.wait()

    own_segment = jnp.sum(
        jnp.where(t_row == t_col, jnp.broadcast_to(seg_buf[me], (tokens, tokens)), 0), axis=1, keepdims=True
    )
    source_segment = jnp.where(own_segment % 2 == 1, own_segment - 1, own_segment)
    for c in range(n_ctx):
        theirs = seg_buf[c]
        allowed = (t_col + c * tokens <= t_row + me * tokens) & (
            (theirs == own_segment) | (theirs == source_segment)
        )
        bias[:, c * tokens : (c + 1) * tokens] = jnp.where(allowed, 0.0, -1e30)

    def relay(s, k, sides=(0, 1)):
        wide = isinstance(k, int) and k < WIDE
        for side in sides:
            origin = z - s if side else z + s
            slot = origin * 2 + core
            valid = (origin >= 0) & (origin < n_z)
            if wide:
                valid &= inner

            @pl.when(valid)
            def _():
                here = piece(k, slot)
                w_mate(here, origin, slot, k).wait_recv()

                @pl.when(takes(side) if wide else has_side(side))
                def _():
                    w_side(side, here, origin, slot, k).start()

                if wide:
                    @pl.when(hub)
                    def _():
                        w_mate(here, origin, slot, k).start()
                else:
                    w_mate(here, origin, slot, k).start()

    scale = HEAD_SIZE ** -0.5 * math.log2(math.e)

    def attend(g, carry):
        lanes = pl.ds(pl.multiple_of(g * HEAD_SIZE, HEAD_SIZE), HEAD_SIZE)

        def heads(i, inner_carry):
            for u in range(HEADS_AT_ONCE):
                head = g * group + i * HEADS_AT_ONCE + u
                at = pl.ds(pl.multiple_of(head * HEAD_SIZE, HEAD_SIZE), HEAD_SIZE)
                scores = lax.dot_general(
                    q_buf[:, at], k_buf[:, lanes], (((1,), (1,)), ((), ())), preferred_element_type=F32
                )
                scores = scores * scale + bias[...]
                peak = jnp.max(scores, axis=1, keepdims=True)
                power = jnp.exp2(scores - peak)
                share = 1.0 / jnp.sum(power, axis=1, keepdims=True)
                mixed = jnp.dot(power.astype(BF16), v_buf[:, lanes], preferred_element_type=F32)
                q_buf[:, at] = (mixed * share).astype(BF16)
            return inner_carry

        lax.fori_loop(0, group // HEADS_AT_ONCE, heads, 0)

        @pl.when((g == 1) & hub)
        def _():
            for j in range(2):
                x_to_hub(j).wait_recv()
            route(0, ids_peer, x_peer)

        for k in range(3):
            @pl.when(g == k + 1)
            def _():
                relay(1, k)

        return carry

    lax.fori_loop(0, KEY_HEAD_COUNT, attend, 0)
    ctx_copy = pltpu.make_async_copy(q_buf, ctx_out, out_sem.at[0])
    ctx_copy.start()
    relay(1, WIDE - 1)

    @pl.when(hub)
    def _():
        for which in (1, 0):
            for d in range(1, n_exp):
                x_arrival(which, d).wait_recv()
    for copy in local[:3]:
        copy.wait()

    def h_back(origin):
        return send(
            hidden.at[0, origin], hidden.at[1, origin], h_send.at[origin], h_recv.at[origin],
            {"ctx": peer * 2 + core},
        )

    def hidden_of(origin):
        other = origin * 2 + 1 - core
        for k in range(WIDE):
            w_mate(piece(k, other), origin, other, k).wait_recv()
        inputs = rows_in[...].reshape(2 * n_exp * cap, width)
        both = pl.ds(origin * 2, 2)
        gate_w = weights[0, both].reshape(-1, width)
        up_w = weights[1, both].reshape(-1, width)
        gate = lax.dot_general(inputs, gate_w, (((1,), (1,)), ((), ())), preferred_element_type=F32)
        up = lax.dot_general(inputs, up_w, (((1,), (1,)), ((), ())), preferred_element_type=F32)
        units = (gate / (1.0 + jnp.exp(-gate)) * up).astype(BF16)
        hidden[0, origin] = units[: n_exp * cap]
        hidden[1, origin] = units[n_exp * cap :]
        h_back(origin).start()

    def own_and_peer(k):
        for side in (0, 1):
            @pl.when(hub & has_side(side) & jnp.logical_not(peer_side(side)))
            def _():
                share_down(side, k)

            @pl.when(peer_side(1 - side))
            def _():
                relay(1, k, (side,))

    def far(s, carry):
        @pl.when(s > 1)
        def _():
            for k in range(WIDE):
                relay(s, k)

        @pl.when(hub)
        def _():
            def one(side, inner_carry):
                origin = z + s - 2 * s * side

                @pl.when((origin >= 0) & (origin < n_z) & ((s > 0) | (side == 0)))
                def _():
                    hidden_of(origin)

                return inner_carry

            lax.fori_loop(0, 2, one, 0)

        @pl.when(s < 2)
        def _():
            def some(i, inner_carry):
                own_and_peer(s * (COLUMN_BLOCKS // 2) + i + WIDE)
                return inner_carry

            lax.fori_loop(0, COLUMN_BLOCKS // 2, some, 0)

        return carry

    lax.fori_loop(0, n_z, far, 0)

    @pl.when(client)
    def _():
        for o in range(n_z):
            h_back(o).wait_recv()
    hidden_all[...] = jnp.concatenate([hidden[1, o] for o in range(n_z)], axis=1)

    def r_out(d, cb):
        there = (mine + d) % n_exp
        return send(
            result.at[there, :, block(cb)], returned.at[mine, :, block(cb)],
            r_send.at[there, cb], r_recv.at[mine, cb], {"exp": there},
        )

    def r_arrival(d, cb):
        source = (mine + d) % n_exp
        return send(
            result.at[source, :, block(cb)], returned.at[source, :, block(cb)],
            r_send.at[source, cb], r_recv.at[source, cb], {"exp": source},
        )

    def mix_copy(cb):
        return pltpu.make_async_copy(mix_buf.at[:, block(cb)], mix_out.at[:, block(cb)], mix_sem.at[cb])

    def combine(cb):
        at = block(cb)
        mix = gates[mine] * jnp.dot(pick[mine], result[mine, :, at], preferred_element_type=F32)
        for d in range(1, n_exp):
            r_arrival(d, cb).wait_recv()
            source = (mine + d) % n_exp
            mix += gates[source] * jnp.dot(pick[source], returned[source, :, at], preferred_element_type=F32)
        mix_buf[:, at] = mix.astype(BF16)
        mix_copy(cb).start()

    def down_block(cb, carry):
        @pl.when(cb < COLUMN_BLOCKS)
        def _():
            k = cb + WIDE

            for side in (0, 1):
                @pl.when(jnp.logical_not(peer_side(1 - side)))
                def _():
                    relay(1, k, (side,))

            def pass_on(s, inner_carry):
                relay(s, k)
                return inner_carry

            lax.fori_loop(2, n_z, pass_on, 0)

            def from_mate(origin, inner_carry):
                other = origin * 2 + 1 - core
                w_mate(piece(k, other), origin, other, k).wait_recv()
                return inner_carry

            lax.fori_loop(0, n_z, from_mate, 0)
            down_w = weights[2, :, :, block(cb)].reshape(-1, columns)
            out = jnp.dot(hidden_all[...], down_w, preferred_element_type=F32)
            result[:, :, block(cb)] = out.astype(BF16).reshape(n_exp, cap, columns)
            for d in range(1, n_exp):
                r_out(d, cb).start()

        @pl.when(cb >= LAG)
        def _():
            combine(cb - LAG)

        return carry

    lax.fori_loop(0, COLUMN_BLOCKS + LAG, down_block, 0)

    @pl.when(has_side(1))
    def _():
        for j in range(3):
            kv_own_up(j).wait_send()
    for j in range(3):
        kv_own_pass(j).wait_send()

    def kv_sent(s, carry):
        origin = z - s

        @pl.when(origin >= 0)
        def _():
            for j in range(3):
                @pl.when(has_side(1))
                def _():
                    kv_up(origin, j).wait_send()

                kv_pass(origin, j).wait_send()

        return carry

    lax.fori_loop(1, n_z, kv_sent, 0)

    def piece_sent(k):
        wide = isinstance(k, int) and k < WIDE
        for side in (0, 1):
            @pl.when(takes(side) if wide else has_side(side))
            def _():
                w_side(side, own_piece(k), z, me, k).wait_send()
        if wide:
            @pl.when(hub)
            def _():
                w_mate(own_piece(k), z, me, k).wait_send()
        else:
            w_mate(own_piece(k), z, me, k).wait_send()

        def passed(s, carry):
            for side in (0, 1):
                origin = z - s if side else z + s
                slot = origin * 2 + core
                valid = (origin >= 0) & (origin < n_z)
                if wide:
                    valid &= inner

                @pl.when(valid)
                def _():
                    here = piece(k, slot)

                    @pl.when(takes(side) if wide else has_side(side))
                    def _():
                        w_side(side, here, origin, slot, k).wait_send()

                    if wide:
                        @pl.when(hub)
                        def _():
                            w_mate(here, origin, slot, k).wait_send()
                    else:
                        w_mate(here, origin, slot, k).wait_send()
            return carry

        lax.fori_loop(1, n_z, passed, 0)

    for k in range(WIDE):
        piece_sent(k)
    each_block(piece_sent)

    @pl.when(client)
    def _():
        for j in range(2):
            x_to_hub(j).wait_send()

    @pl.when(hub)
    def _():
        for which in (0, 1):
            for d in range(1, n_exp):
                x_out(which, d).wait_send()
        for o in range(n_z):
            h_back(o).wait_send()

    def results_sent(cb, carry):
        for d in range(1, n_exp):
            r_out(d, cb).wait_send()
        mix_copy(cb).wait()
        return carry

    lax.fori_loop(0, COLUMN_BLOCKS, results_sent, 0)
    ctx_copy.wait()


def on_device(
    n_ctx, n_exp,
    queries, key_head_vectors, value_head_vectors, segment_ids,
    normed, expert_ids, gate_probs, gate_weight, up_weight, down_weight,
):
    tokens, q_width = queries.shape[1:]
    kv_width = key_head_vectors.shape[2]
    width = normed.shape[2]
    hidden = gate_weight.shape[1]
    most = tokens * expert_ids.shape[2] * 5 // (4 * n_exp)
    cap = -(-most // 16) * 16
    span = n_ctx * tokens
    n_z = n_ctx // 2
    dma = pltpu.SemaphoreType.DMA
    hbm = pl.BlockSpec(memory_space=pl.ANY)
    vmem = pl.BlockSpec(memory_space=pltpu.VMEM)
    context, mixture = pl.pallas_call(
        functools.partial(kernel, n_ctx, n_exp, cap),
        out_shape=(
            jax.ShapeDtypeStruct((tokens, q_width), BF16),
            jax.ShapeDtypeStruct((tokens, width), BF16),
        ),
        in_specs=[hbm, hbm, hbm, vmem, vmem, vmem, vmem, hbm, hbm, hbm],
        out_specs=(hbm, hbm),
        scratch_shapes=[
            pltpu.VMEM((tokens, q_width), BF16),
            pltpu.VMEM((span, kv_width), BF16),
            pltpu.VMEM((span, kv_width), BF16),
            pltpu.VMEM((n_ctx, 1, tokens), jnp.int32),
            pltpu.VMEM((tokens, span), F32),
            pltpu.VMEM((3, n_ctx, hidden, width), BF16),
            pltpu.VMEM((tokens, width), BF16),
            pltpu.VMEM((expert_ids.shape[2], tokens), jnp.int32),
            pltpu.VMEM((2, n_exp, cap, width), BF16),
            pltpu.VMEM((2, n_exp, cap, width), BF16),
            pltpu.VMEM((2, n_z, n_exp * cap, 2 * hidden), BF16),
            pltpu.VMEM((n_exp * cap, n_ctx * hidden), BF16),
            pltpu.VMEM((n_exp, cap, width), BF16),
            pltpu.VMEM((n_exp, cap, width), BF16),
            pltpu.VMEM((n_exp, tokens, cap), BF16),
            pltpu.VMEM((n_exp, tokens, 1), F32),
            pltpu.VMEM((tokens, width), BF16),
            dma((7,)),
            dma((n_z, 3)),
            dma((n_z, 3)),
            dma((n_ctx, 3)),
            dma((n_z, PIECES)),
            dma((n_z, PIECES)),
            dma((n_z, PIECES)),
            dma((n_ctx, PIECES)),
            dma((2,)),
            dma((2,)),
            dma((2, n_exp)),
            dma((2, n_exp)),
            dma((n_z,)),
            dma((n_z,)),
            dma((n_exp, COLUMN_BLOCKS)),
            dma((n_exp, COLUMN_BLOCKS)),
            dma((1,)),
            dma((COLUMN_BLOCKS,)),
        ],
        compiler_params=pltpu.CompilerParams(
            collective_id=0, has_side_effects=True, vmem_limit_bytes=60 * 1024 * 1024
        ),
        name="layer",
    )(
        queries[0], key_head_vectors[0], value_head_vectors[0], segment_ids,
        normed[0], expert_ids[0].T, gate_probs[0].T, gate_weight[0], up_weight[0], down_weight[0],
    )
    return context[None], mixture[None]


def solution(mesh):
    rows = P("exp", "ctx", None)
    in_specs = (rows, rows, rows, P("exp", "ctx"), rows, rows, rows, rows, rows, rows)
    return jax.shard_map(
        functools.partial(on_device, mesh.shape["ctx"], mesh.shape["exp"]),
        mesh=mesh, in_specs=in_specs, out_specs=(rows, rows), check_vma=False,
    )
```

```python
import functools
import math

import jax
import jax.numpy as jnp
from jax import lax
from jax.experimental import pallas as pl
from jax.experimental.pallas import tpu as pltpu
from jax.sharding import PartitionSpec as P

KEY_HEAD_COUNT = 4
HEAD_SIZE = 128
COLUMN_BLOCKS = 8
HEADS_AT_ONCE = 4
HALVES = 2
WIDE = 2 * HALVES
LAG = 2
MESH = pl.DeviceIdType.MESH
F32 = jnp.float32
BF16 = jnp.bfloat16


def kernel(
    n_ctx, n_exp, cap,
    q_hbm, k_hbm, v_hbm, seg_in, x_in, ids_in, prob_in, gate_hbm, up_hbm, down_hbm,
    ctx_out, mix_out,
    q_buf, kv_buf, seg_buf, bias, weights, x_peer, ids_peer, rows_out, rows_in,
    hidden, hidden_all, result, returned, pick, gates, mix_buf,
    local_sem, kv_send, kv_swap, kv_recv, w_send, w_recv, w_swapped,
    d_send, d_recv, d_swap, d_swapped, u_send, u_recv, u_swap, u_swapped,
    t_send, t_recv, x_send, x_recv, h_send, h_recv, r_send, r_recv, out_sem,
):
    me = lax.axis_index("ctx")
    mine = lax.axis_index("exp")
    n_z = n_ctx // 2
    n_pair = n_z // 2
    z, core = me // 2, me % 2
    other = 1 - core
    mate = me + 1 - 2 * core
    toward = 1 - 2 * (z % 2)
    peer = z + toward
    pair = z // 2
    hub = jnp.where(z < n_z // 2, z % 2 == 1, z % 2 == 0)
    client = jnp.logical_not(hub)
    inner = (z > 0) & (z < n_z - 1)
    tokens, width = x_in.shape
    group = q_buf.shape[1] // (KEY_HEAD_COUNT * HEAD_SIZE)
    columns = width // COLUMN_BLOCKS
    half = width // HALVES

    def send(src, dst, send_sem, recv_sem, where):
        return pltpu.make_async_remote_copy(
            src_ref=src, dst_ref=dst, send_sem=send_sem, recv_sem=recv_sem,
            device_id=where, device_id_type=MESH,
        )

    to_mate = {"ctx": mate}
    to_peer = {"ctx": peer * 2 + core}

    def to_side(side):
        return {"ctx": me + 2 if side else me - 2}

    def block(cb):
        return pl.ds(pl.multiple_of(cb * columns, columns), columns)

    def has_side(side):
        return z + 1 < n_z if side else z > 0

    def takes(side):
        return z + 1 < n_z - 1 if side else z > 1

    def peer_side(side):
        return z % 2 == 1 - side

    barrier = pltpu.get_barrier_semaphore()
    for side in (0, 1):
        @pl.when(has_side(side))
        def _():
            pl.semaphore_signal(barrier, inc=1, device_id=to_side(side), device_id_type=MESH)
    pl.semaphore_signal(barrier, inc=1, device_id=to_mate, device_id_type=MESH)
    for d in range(1, n_exp):
        pl.semaphore_signal(barrier, inc=1, device_id={"exp": (mine + d) % n_exp}, device_id_type=MESH)
    pl.semaphore_wait(barrier, n_exp + jnp.where(inner, 2, 1))

    def kv_rows(slot):
        return kv_buf.at[:, pl.ds(pl.multiple_of(slot * tokens, tokens), tokens)]

    def kv_copies(origin, sem, where, own=False):
        slot = origin * 2 + core
        rows = pl.ds(pl.multiple_of(slot * tokens, tokens), tokens)
        if own:
            pairs = [(k_hbm, kv_buf.at[0, rows], 0), (v_hbm, kv_buf.at[1, rows], 0), (seg_in, seg_buf.at[slot], 1)]
        else:
            pairs = [(kv_rows(slot), kv_rows(slot), 0), (seg_buf.at[slot], seg_buf.at[slot], 1)]
        return [send(src, dst, sem.at[origin, j], kv_recv.at[slot, j], where) for src, dst, j in pairs]

    def kv_wait(slot, sems):
        refs = (kv_rows(slot), seg_buf.at[slot])
        return [send(refs[j], refs[j], sems.at[j], sems.at[j], to_mate) for j in range(2)]

    @pl.when(has_side(1))
    def _():
        for copy in kv_copies(z, kv_send, to_side(1), own=True):
            copy.start()
    for copy in kv_copies(z, kv_swap, to_mate, own=True):
        copy.start()

    def wide_own(k):
        return (gate_hbm, up_hbm)[k // HALVES].at[:, pl.ds(k % HALVES * half, half)]

    def wide_piece(k, origin):
        return weights.at[k // HALVES, origin, core, :, pl.ds(k % HALVES * half, half)]

    def wide_side(side, src, origin, k):
        return send(src, wide_piece(k, origin), w_send.at[side, origin], w_recv.at[origin, k], to_side(side))

    def wide_mate(src, origin, k):
        return send(src, wide_piece(k, origin), w_send.at[2, origin], w_swapped.at[origin], to_mate)

    def wide_all(origin, which, sem):
        ref = weights.at[pl.ds(0, 2), origin, which]
        return send(ref, ref, sem, sem, to_mate)

    def share_wide(side):
        @pl.when(takes(side))
        def _():
            for k in range(WIDE):
                wide_side(side, wide_own(k), z, k).start()

    def x_to_hub(j):
        src, dst = ((ids_in, ids_peer), (x_in, x_peer))[j]
        return send(src, dst, t_send.at[j], t_recv.at[j], to_peer)

    @pl.when(client)
    def _():
        for j in range(2):
            x_to_hub(j).start()
        share_wide(1)
    share_wide(0)

    d_half = width // 2

    def down_own(i):
        cols = pl.ds(pl.multiple_of(i * d_half, d_half), d_half)
        return send(
            down_hbm.at[:, cols], weights.at[2, z, core, :, cols], d_send.at[0], d_recv.at[i], to_peer
        )

    def down_peer(i):
        cols = pl.ds(pl.multiple_of(i * d_half, d_half), d_half)
        here = weights.at[2, peer, core, :, cols]
        return send(here, here, d_swap.at[0], d_recv.at[i], to_mate)

    def down_own_mate():
        return send(down_hbm, weights.at[2, z, core], d_swap.at[0], d_swapped.at[0], to_mate)

    def down_peer_mate(i):
        cols = pl.ds(pl.multiple_of(i * d_half, d_half), d_half)
        here = weights.at[2, peer, core, :, cols]
        return send(here, here, d_swap.at[0], d_swapped.at[0], to_mate)

    def unit(q, which, cols=slice(None)):
        return weights.at[2, pl.ds(q * 2, 2), which, :, cols]

    def unit_side(side, q, cb):
        ref = unit(q, core, block(cb))
        return send(ref, ref, u_send.at[q], u_recv.at[q, cb], to_side(side))

    def unit_mate(q, cb):
        ref = unit(q, core, block(cb))
        return send(ref, ref, u_swap.at[q], u_swapped.at[q, cb], to_mate)

    def unit_from_mate(q, cb):
        ref = unit(q, other, block(cb))
        return send(ref, ref, u_swap.at[q], u_swapped.at[q, cb], to_mate)

    for i in range(2):
        down_own(i).start()

    @pl.when(hub)
    def _():
        for k in range(WIDE):
            wide_mate(wide_own(k), z, k).start()
    down_own_mate().start()

    local = [
        pltpu.make_async_copy(w, weights.at[k, z, core], local_sem.at[k])
        for k, w in enumerate((gate_hbm, up_hbm, down_hbm))
    ]
    my_rows = pl.ds(pl.multiple_of(me * tokens, tokens), tokens)
    local += [
        pltpu.make_async_copy(k_hbm, kv_buf.at[0, my_rows], local_sem.at[3]),
        pltpu.make_async_copy(v_hbm, kv_buf.at[1, my_rows], local_sem.at[4]),
        pltpu.make_async_copy(seg_in, seg_buf.at[me], local_sem.at[5]),
        pltpu.make_async_copy(q_hbm, q_buf, local_sem.at[6]),
    ]
    for copy in local:
        copy.start()

    t_row = lax.broadcasted_iota(jnp.int32, (tokens, tokens), 0)
    t_col = lax.broadcasted_iota(jnp.int32, (tokens, tokens), 1)

    def as_column(row):
        return jnp.sum(jnp.where(t_row == t_col, row, jnp.zeros_like(row)), axis=1, keepdims=True)

    def x_out(which, d):
        there = (mine + d) % n_exp
        return send(
            rows_out.at[which, there], rows_in.at[which, d], x_send.at[which], x_recv.at[which], {"exp": there}
        )

    def x_all(which):
        ref = rows_in.at[which, pl.ds(1, n_exp - 1)]
        return send(ref, ref, x_send.at[which], x_recv.at[which], to_mate)

    def route(which, ids_ref, x_ref):
        ids = ids_ref[...]
        row0, row1 = ids[0:1, :], ids[1:2, :]
        e_row = lax.broadcasted_iota(jnp.int32, (n_exp, tokens), 0)
        named_row = jnp.where((e_row == row0) | (e_row == row1), 1.0, 0.0).astype(F32)
        after = jnp.where(t_row < t_col, 1.0, 0.0).astype(BF16)
        rank_row = jnp.dot(named_row.astype(BF16), after, preferred_element_type=F32)
        place_row = lax.broadcasted_iota(jnp.int32, (cap, tokens), 0).astype(F32)
        x = x_ref[...]
        for e in range(n_exp):
            chosen = jnp.where(place_row == rank_row[e : e + 1, :], named_row[e : e + 1, :], 0.0)
            rows_out[which, e] = jnp.dot(chosen.astype(BF16), x, preferred_element_type=F32).astype(BF16)
        for d in range(1, n_exp):
            x_out(which, d).start()
        rows_in[which, 0] = rows_out[which, mine]

    @pl.when(hub)
    def _():
        route(1, ids_in, x_in)

    def kv_relay(s, carry):
        origin = z - s

        @pl.when(origin >= 0)
        def _():
            slot = origin * 2 + core
            for copy in kv_wait(slot, kv_recv.at[slot]):
                copy.wait_recv()

            @pl.when(has_side(1))
            def _():
                for copy in kv_copies(origin, kv_send, to_side(1)):
                    copy.start()

            for copy in kv_copies(origin, kv_swap, to_mate):
                copy.start()

        return carry

    lax.fori_loop(1, n_z, kv_relay, 0)

    @pl.when(hub)
    def _():
        share_wide(1)

    ids = ids_in[...]
    probs = prob_in[...]
    id0, id1 = as_column(ids[0:1, :]), as_column(ids[1:2, :])
    e_col = lax.broadcasted_iota(jnp.int32, (tokens, n_exp), 1)
    named_col = jnp.where((e_col == id0) | (e_col == id1), 1.0, 0.0).astype(F32)
    before = jnp.where(t_col < t_row, 1.0, 0.0).astype(BF16)
    rank_col = jnp.dot(before, named_col.astype(BF16), preferred_element_type=F32)
    weight_col = jnp.where(e_col == id0, as_column(probs[0:1, :]), 0.0) + jnp.where(
        e_col == id1, as_column(probs[1:2, :]), 0.0
    )
    place_col = lax.broadcasted_iota(jnp.int32, (tokens, cap), 1).astype(F32)
    for e in range(n_exp):
        back = jnp.where(place_col == rank_col[:, e : e + 1], named_col[:, e : e + 1], 0.0)
        pick[e] = back.astype(BF16)
        gates[e] = weight_col[:, e : e + 1]

    def kv_from_mate(origin, carry):
        @pl.when(origin <= z)
        def _():
            slot = origin * 2 + other
            for copy in kv_wait(slot, kv_recv.at[slot]):
                copy.wait_recv()

        @pl.when(origin > z)
        def _():
            both = pl.ds(pl.multiple_of(origin * 2 * tokens, 2 * tokens), 2 * tokens)
            kv_buf[:, both] = jnp.zeros((2, 2 * tokens, kv_buf.shape[2]), BF16)
            seg_buf[pl.ds(origin * 2, 2)] = jnp.zeros((2, 1, tokens), jnp.int32)

        return carry

    lax.fori_loop(0, n_z, kv_from_mate, 0)
    for copy in local[3:]:
        copy.wait()

    own_segment = jnp.sum(
        jnp.where(t_row == t_col, jnp.broadcast_to(seg_buf[me], (tokens, tokens)), 0), axis=1, keepdims=True
    )
    source_segment = jnp.where(own_segment % 2 == 1, own_segment - 1, own_segment)
    for c in range(n_ctx):
        theirs = seg_buf[c]
        allowed = (t_col + c * tokens <= t_row + me * tokens) & (
            (theirs == own_segment) | (theirs == source_segment)
        )
        bias[:, c * tokens : (c + 1) * tokens] = jnp.where(allowed, 0.0, -1e30)

    def relay_wide(s, k):
        for side in (0, 1):
            origin = z - s if side else z + s

            @pl.when((origin >= 0) & (origin < n_z) & inner)
            def _():
                here = wide_piece(k, origin)
                wide_side(side, here, origin, k).wait_recv()

                @pl.when(takes(side))
                def _():
                    wide_side(side, here, origin, k).start()

                @pl.when(hub)
                def _():
                    wide_mate(here, origin, k).start()

    scale = HEAD_SIZE ** -0.5 * math.log2(math.e)

    def attend(g, carry):
        lanes = pl.ds(pl.multiple_of(g * HEAD_SIZE, HEAD_SIZE), HEAD_SIZE)

        def heads(i, inner_carry):
            for u in range(HEADS_AT_ONCE):
                head = g * group + i * HEADS_AT_ONCE + u
                at = pl.ds(pl.multiple_of(head * HEAD_SIZE, HEAD_SIZE), HEAD_SIZE)
                scores = lax.dot_general(
                    q_buf[:, at], kv_buf[0, :, lanes], (((1,), (1,)), ((), ())), preferred_element_type=F32
                )
                scores = scores * scale + bias[...]
                peak = jnp.max(scores, axis=1, keepdims=True)
                power = jnp.exp2(scores - peak)
                share = 1.0 / jnp.sum(power, axis=1, keepdims=True)
                mixed = jnp.dot(power.astype(BF16), kv_buf[1, :, lanes], preferred_element_type=F32)
                q_buf[:, at] = (mixed * share).astype(BF16)
            return inner_carry

        lax.fori_loop(0, group // HEADS_AT_ONCE, heads, 0)

        @pl.when((g == 1) & hub)
        def _():
            for j in range(2):
                x_to_hub(j).wait_recv()
            route(0, ids_peer, x_peer)

        for k in range(WIDE):
            @pl.when(g == min(k + 1, KEY_HEAD_COUNT - 1))
            def _():
                relay_wide(1, k)

        return carry

    lax.fori_loop(0, KEY_HEAD_COUNT, attend, 0)
    ctx_copy = pltpu.make_async_copy(q_buf, ctx_out, out_sem.at[0])
    ctx_copy.start()

    @pl.when(hub)
    def _():
        for which in (1, 0):
            x_all(which).wait_recv()
    for copy in local[:3]:
        copy.wait()

    def h_back(origin):
        return send(hidden.at[0, origin], hidden.at[1, origin], h_send.at[0], h_recv.at[0], to_peer)

    h_all = send(hidden.at[0], hidden.at[1], h_send.at[0], h_recv.at[0], to_peer)

    def hidden_of(origin):
        wide_all(origin, other, w_swapped.at[origin]).wait_recv()
        inputs = rows_in[...].reshape(2 * n_exp * cap, width)
        gate_w = weights[0, origin].reshape(-1, width)
        up_w = weights[1, origin].reshape(-1, width)
        gate = lax.dot_general(inputs, gate_w, (((1,), (1,)), ((), ())), preferred_element_type=F32)
        up = lax.dot_general(inputs, up_w, (((1,), (1,)), ((), ())), preferred_element_type=F32)
        units = (gate / (1.0 + jnp.exp(-gate)) * up).astype(BF16)
        hidden[0, origin] = units[: n_exp * cap]
        hidden[1, origin] = units[n_exp * cap :]
        h_back(origin).start()

    def pair_half(i):
        down_peer(i).wait_recv()
        per = COLUMN_BLOCKS // 2
        for side in (0, 1):
            @pl.when(has_side(side) & jnp.logical_not(peer_side(side)))
            def _():
                for c in range(per):
                    unit_side(side, pair, i * per + c).start()
        down_peer_mate(i).start()

    def far(t, carry):
        s = (t + 1) // 2
        origin = z + jnp.where(t % 2 == 1, -toward, toward) * s

        for i in range(2):
            @pl.when(t == 2 + i)
            def _():
                pair_half(i)

        @pl.when((t % 2 == 1) & (s > 1))
        def _():
            for k in range(WIDE):
                relay_wide(s, k)

        @pl.when(hub & (origin >= 0) & (origin < n_z))
        def _():
            hidden_of(origin)

        return carry

    lax.fori_loop(0, 2 * n_z - 1, far, 0)

    @pl.when(client)
    def _():
        h_all.wait_recv()
    hidden_all[...] = jnp.concatenate([hidden[1, o] for o in range(n_z)], axis=1)
    own_unit = unit(pair, other)
    send(own_unit, own_unit, d_swap.at[0], d_swapped.at[0], to_mate).wait_recv()

    def r_out(d, cb):
        return send(
            result.at[d, :, block(cb)], returned.at[d - 1, :, block(cb)],
            r_send.at[0], r_recv.at[cb], {"exp": (mine + n_exp - d) % n_exp},
        )

    def r_block(cb):
        ref = returned.at[:, :, block(cb)]
        return send(ref, ref, r_send.at[0], r_recv.at[cb], to_mate)

    def mix_copy(cb):
        return pltpu.make_async_copy(mix_buf.at[:, block(cb)], mix_out.at[:, block(cb)], out_sem.at[1])

    def combine(cb):
        at = block(cb)
        mix = gates[mine] * jnp.dot(pick[mine], result[0, :, at], preferred_element_type=F32)
        r_block(cb).wait_recv()
        for d in range(1, n_exp):
            source = (mine + d) % n_exp
            mix += gates[source] * jnp.dot(pick[source], returned[d - 1, :, at], preferred_element_type=F32)
        mix_buf[:, at] = mix.astype(BF16)
        mix_copy(cb).start()

    def each_other(what):
        def one(s, carry):
            for side in (0, 1):
                q = pair - s if side else pair + s

                @pl.when((q >= 0) & (q < n_pair))
                def _():
                    what(side, q)

            return carry

        lax.fori_loop(1, n_pair, one, 0)

    def early_sends():
        @pl.when(has_side(1))
        def _():
            for copy in kv_wait(me, kv_send.at[z]):
                copy.wait_send()
        for copy in kv_wait(me, kv_swap.at[z]):
            copy.wait_send()

        def kv_sent(s, carry):
            origin = z - s

            @pl.when(origin >= 0)
            def _():
                @pl.when(has_side(1))
                def _():
                    for copy in kv_wait(origin * 2 + core, kv_send.at[origin]):
                        copy.wait_send()

                for copy in kv_wait(origin * 2 + core, kv_swap.at[origin]):
                    copy.wait_send()

            return carry

        lax.fori_loop(1, n_z, kv_sent, 0)

        @pl.when(client)
        def _():
            for j in range(2):
                x_to_hub(j).wait_send()

        @pl.when(hub)
        def _():
            for which in (0, 1):
                x_all(which).wait_send()
            h_all.wait_send()

        def wide_sent(origin, carry):
            for side in (0, 1):
                @pl.when(takes(side) & ((origin == z) | (inner & (origin < z if side else origin > z))))
                def _():
                    wide_all(origin, core, w_send.at[side, origin]).wait_send()

            @pl.when(hub)
            def _():
                wide_all(origin, core, w_send.at[2, origin]).wait_send()

            return carry

        lax.fori_loop(0, n_z, wide_sent, 0)
        d_all = weights.at[2, z, core]
        send(d_all, d_all, d_send.at[0], d_recv.at[0], to_mate).wait_send()
        swapped = unit(pair, core)
        send(swapped, swapped, d_swap.at[0], d_swapped.at[0], to_mate).wait_send()

    def down_block(cb, carry):
        @pl.when(cb < COLUMN_BLOCKS)
        def _():
            def pass_on(side, q):
                unit_side(side, q, cb).wait_recv()

                @pl.when(has_side(side))
                def _():
                    unit_side(side, q, cb).start()

                unit_mate(q, cb).start()

            each_other(pass_on)
            each_other(lambda side, q: unit_from_mate(q, cb).wait_recv())
            down_w = weights[2, :, :, :, block(cb)].reshape(-1, columns)
            out = jnp.dot(hidden_all[...], down_w, preferred_element_type=F32)
            result[:, :, block(cb)] = out.astype(BF16).reshape(n_exp, cap, columns)
            for d in range(1, n_exp):
                r_out(d, cb).start()

        @pl.when(cb >= LAG)
        def _():
            combine(cb - LAG)

        @pl.when(cb == LAG)
        def _():
            early_sends()

        return carry

    lax.fori_loop(0, COLUMN_BLOCKS + LAG, down_block, 0)

    for side in (0, 1):
        @pl.when(has_side(side) & jnp.logical_not(peer_side(side)))
        def _():
            ref = unit(pair, core)
            send(ref, ref, u_send.at[pair], u_send.at[pair], to_mate).wait_send()

    def units_sent(side, q):
        ref = unit(q, core)

        @pl.when(has_side(side))
        def _():
            send(ref, ref, u_send.at[q], u_send.at[q], to_mate).wait_send()

        send(ref, ref, u_swap.at[q], u_swap.at[q], to_mate).wait_send()

    each_other(units_sent)
    send(returned, returned, r_send.at[0], r_send.at[0], to_mate).wait_send()
    pltpu.make_async_copy(mix_buf, mix_out, out_sem.at[1]).wait()
    ctx_copy.wait()


def on_device(
    n_ctx, n_exp,
    queries, key_head_vectors, value_head_vectors, segment_ids,
    normed, expert_ids, gate_probs, gate_weight, up_weight, down_weight,
):
    tokens, q_width = queries.shape[1:]
    kv_width = key_head_vectors.shape[2]
    width = normed.shape[2]
    hidden = gate_weight.shape[1]
    most = tokens * expert_ids.shape[2] * 5 // (4 * n_exp)
    cap = -(-most // 16) * 16
    span = n_ctx * tokens
    n_z = n_ctx // 2
    dma = pltpu.SemaphoreType.DMA
    hbm = pl.BlockSpec(memory_space=pl.ANY)
    vmem = pl.BlockSpec(memory_space=pltpu.VMEM)
    context, mixture = pl.pallas_call(
        functools.partial(kernel, n_ctx, n_exp, cap),
        out_shape=(
            jax.ShapeDtypeStruct((tokens, q_width), BF16),
            jax.ShapeDtypeStruct((tokens, width), BF16),
        ),
        in_specs=[hbm, hbm, hbm, vmem, vmem, vmem, vmem, hbm, hbm, hbm],
        out_specs=(hbm, hbm),
        scratch_shapes=[
            pltpu.VMEM((tokens, q_width), BF16),
            pltpu.VMEM((2, span, kv_width), BF16),
            pltpu.VMEM((n_ctx, 1, tokens), jnp.int32),
            pltpu.VMEM((tokens, span), F32),
            pltpu.VMEM((3, n_z, 2, hidden, width), BF16),
            pltpu.VMEM((tokens, width), BF16),
            pltpu.VMEM((expert_ids.shape[2], tokens), jnp.int32),
            pltpu.VMEM((2, n_exp, cap, width), BF16),
            pltpu.VMEM((2, n_exp, cap, width), BF16),
            pltpu.VMEM((2, n_z, n_exp * cap, 2 * hidden), BF16),
            pltpu.VMEM((n_exp * cap, n_ctx * hidden), BF16),
            pltpu.VMEM((n_exp, cap, width), BF16),
            pltpu.VMEM((n_exp - 1, cap, width), BF16),
            pltpu.VMEM((n_exp, tokens, cap), BF16),
            pltpu.VMEM((n_exp, tokens, 1), F32),
            pltpu.VMEM((tokens, width), BF16),
            dma((7,)),
            dma((n_z, 2)),
            dma((n_z, 2)),
            dma((n_ctx, 2)),
            dma((3, n_z)),
            dma((n_z, WIDE)),
            dma((n_z,)),
            dma((1,)),
            dma((2,)),
            dma((1,)),
            dma((1,)),
            dma((n_z // 2,)),
            dma((n_z // 2, COLUMN_BLOCKS)),
            dma((n_z // 2,)),
            dma((n_z // 2, COLUMN_BLOCKS)),
            dma((2,)),
            dma((2,)),
            dma((2,)),
            dma((2,)),
            dma((1,)),
            dma((1,)),
            dma((1,)),
            dma((COLUMN_BLOCKS,)),
            dma((2,)),
        ],
        compiler_params=pltpu.CompilerParams(
            collective_id=0, has_side_effects=True, vmem_limit_bytes=60 * 1024 * 1024
        ),
        name="layer",
    )(
        queries[0], key_head_vectors[0], value_head_vectors[0], segment_ids,
        normed[0], expert_ids[0].T, gate_probs[0].T, gate_weight[0], up_weight[0], down_weight[0],
    )
    return context[None], mixture[None]


def solution(mesh):
    rows = P("exp", "ctx", None)
    in_specs = (rows, rows, rows, P("exp", "ctx"), rows, rows, rows, rows, rows, rows)
    return jax.shard_map(
        functools.partial(on_device, mesh.shape["ctx"], mesh.shape["exp"]),
        mesh=mesh, in_specs=in_specs, out_specs=(rows, rows), check_vma=False,
    )
```

```python
import functools
import math

import jax
import jax.numpy as jnp
from jax import lax
from jax.experimental import pallas as pl
from jax.experimental.pallas import tpu as pltpu
from jax.sharding import PartitionSpec as P

KEY_HEAD_COUNT = 4
HEAD_SIZE = 128
COLUMN_BLOCKS = 8
HEADS_AT_ONCE = 4
HALVES = 2
WIDE = 2 * HALVES
LAG = 2
MESH = pl.DeviceIdType.MESH
F32 = jnp.float32
BF16 = jnp.bfloat16


def kernel(
    n_ctx, n_exp, cap,
    q_hbm, k_hbm, v_hbm, seg_in, x_in, ids_in, prob_in, gate_hbm, up_hbm, down_hbm,
    ctx_out, mix_out,
    q_buf, kv_buf, seg_buf, bias, weights, x_peer, ids_peer, rows_out, rows_in,
    hidden, hidden_all, result, returned, pick, gates, mix_buf,
    local_sem, kv_send, kv_swap, kv_recv, w_send, w_recv, w_swapped,
    d_send, d_recv, d_swap, d_swapped, u_send, u_recv, u_swap, u_swapped,
    t_send, t_recv, x_send, x_recv, h_send, h_recv, r_send, r_recv, out_sem,
):
    me = lax.axis_index("ctx")
    mine = lax.axis_index("exp")
    n_z = n_ctx // 2
    n_pair = n_z // 2
    z, core = me // 2, me % 2
    other = 1 - core
    mate = me + 1 - 2 * core
    toward = 1 - 2 * (z % 2)
    peer = z + toward
    pair = z // 2
    hub = jnp.where(z < n_z // 2, z % 2 == 1, z % 2 == 0)
    client = jnp.logical_not(hub)
    inner = (z > 0) & (z < n_z - 1)
    tokens, width = x_in.shape
    group = q_buf.shape[1] // (KEY_HEAD_COUNT * HEAD_SIZE)
    columns = width // COLUMN_BLOCKS
    half = width // HALVES

    def send(src, dst, send_sem, recv_sem, where):
        return pltpu.make_async_remote_copy(
            src_ref=src, dst_ref=dst, send_sem=send_sem, recv_sem=recv_sem,
            device_id=where, device_id_type=MESH,
        )

    to_mate = {"ctx": mate}
    to_peer = {"ctx": peer * 2 + core}

    def to_side(side):
        return {"ctx": me + 2 if side else me - 2}

    def block(cb):
        return pl.ds(pl.multiple_of(cb * columns, columns), columns)

    def has_side(side):
        return z + 1 < n_z if side else z > 0

    def takes(side):
        return z + 1 < n_z - 1 if side else z > 1

    def peer_side(side):
        return z % 2 == 1 - side

    barrier = pltpu.get_barrier_semaphore()
    for side in (0, 1):
        @pl.when(has_side(side))
        def _():
            pl.semaphore_signal(barrier, inc=1, device_id=to_side(side), device_id_type=MESH)
    pl.semaphore_signal(barrier, inc=1, device_id=to_mate, device_id_type=MESH)
    for d in range(1, n_exp):
        pl.semaphore_signal(barrier, inc=1, device_id={"exp": (mine + d) % n_exp}, device_id_type=MESH)
    pl.semaphore_wait(barrier, n_exp + jnp.where(inner, 2, 1))

    def kv_rows(slot):
        return kv_buf.at[:, pl.ds(pl.multiple_of(slot * tokens, tokens), tokens)]

    def kv_copies(origin, sem, where, own=False):
        slot = origin * 2 + core
        rows = pl.ds(pl.multiple_of(slot * tokens, tokens), tokens)
        if own:
            pairs = [(k_hbm, kv_buf.at[0, rows], 0), (v_hbm, kv_buf.at[1, rows], 0), (seg_in, seg_buf.at[slot], 1)]
        else:
            pairs = [(kv_rows(slot), kv_rows(slot), 0), (seg_buf.at[slot], seg_buf.at[slot], 1)]
        return [send(src, dst, sem.at[origin, j], kv_recv.at[slot, j], where) for src, dst, j in pairs]

    def kv_wait(slot, sems):
        refs = (kv_rows(slot), seg_buf.at[slot])
        return [send(refs[j], refs[j], sems.at[j], sems.at[j], to_mate) for j in range(2)]

    @pl.when(has_side(1))
    def _():
        for copy in kv_copies(z, kv_send, to_side(1), own=True):
            copy.start()
    for copy in kv_copies(z, kv_swap, to_mate, own=True):
        copy.start()

    def wide_own(k):
        return (gate_hbm, up_hbm)[k // HALVES].at[:, pl.ds(k % HALVES * half, half)]

    def wide_piece(k, origin):
        return weights.at[k // HALVES, origin, core, :, pl.ds(k % HALVES * half, half)]

    def wide_side(side, src, origin, k):
        return send(src, wide_piece(k, origin), w_send.at[side, origin], w_recv.at[origin, k], to_side(side))

    def wide_mate(src, origin, k):
        return send(src, wide_piece(k, origin), w_send.at[2, origin], w_swapped.at[origin], to_mate)

    def wide_all(origin, which, sem):
        ref = weights.at[pl.ds(0, 2), origin, which]
        return send(ref, ref, sem, sem, to_mate)

    def share_wide(side):
        @pl.when(takes(side))
        def _():
            for k in range(WIDE):
                wide_side(side, wide_own(k), z, k).start()

    def x_to_hub(j):
        src, dst = ((ids_in, ids_peer), (x_in, x_peer))[j]
        return send(src, dst, t_send.at[j], t_recv.at[j], to_peer)

    @pl.when(client)
    def _():
        for j in range(2):
            x_to_hub(j).start()
        share_wide(1)
    share_wide(0)

    d_half = width // 2

    def down_own(i):
        cols = pl.ds(pl.multiple_of(i * d_half, d_half), d_half)
        return send(
            down_hbm.at[:, cols], weights.at[2, z, core, :, cols], d_send.at[0], d_recv.at[i], to_peer
        )

    def down_peer(i):
        cols = pl.ds(pl.multiple_of(i * d_half, d_half), d_half)
        here = weights.at[2, peer, core, :, cols]
        return send(here, here, d_swap.at[0], d_recv.at[i], to_mate)

    def down_own_mate():
        return send(down_hbm, weights.at[2, z, core], d_swap.at[0], d_swapped.at[0], to_mate)

    def down_peer_mate(i):
        cols = pl.ds(pl.multiple_of(i * d_half, d_half), d_half)
        here = weights.at[2, peer, core, :, cols]
        return send(here, here, d_swap.at[0], d_swapped.at[0], to_mate)

    def unit(q, which, cols=slice(None)):
        return weights.at[2, pl.ds(q * 2, 2), which, :, cols]

    def unit_side(side, q, cb):
        ref = unit(q, core, block(cb))
        return send(ref, ref, u_send.at[q], u_recv.at[q, cb], to_side(side))

    def unit_mate(q, cb):
        ref = unit(q, core, block(cb))
        return send(ref, ref, u_swap.at[q], u_swapped.at[q, cb], to_mate)

    def unit_from_mate(q, cb):
        ref = unit(q, other, block(cb))
        return send(ref, ref, u_swap.at[q], u_swapped.at[q, cb], to_mate)

    for i in range(2):
        down_own(i).start()

    @pl.when(hub)
    def _():
        for k in range(WIDE):
            wide_mate(wide_own(k), z, k).start()
    down_own_mate().start()

    local = [
        pltpu.make_async_copy(w, weights.at[k, z, core], local_sem.at[k])
        for k, w in enumerate((gate_hbm, up_hbm, down_hbm))
    ]
    my_rows = pl.ds(pl.multiple_of(me * tokens, tokens), tokens)
    local += [
        pltpu.make_async_copy(k_hbm, kv_buf.at[0, my_rows], local_sem.at[3]),
        pltpu.make_async_copy(v_hbm, kv_buf.at[1, my_rows], local_sem.at[4]),
        pltpu.make_async_copy(seg_in, seg_buf.at[me], local_sem.at[5]),
        pltpu.make_async_copy(q_hbm, q_buf, local_sem.at[6]),
    ]
    for copy in local:
        copy.start()

    t_row = lax.broadcasted_iota(jnp.int32, (tokens, tokens), 0)
    t_col = lax.broadcasted_iota(jnp.int32, (tokens, tokens), 1)

    def as_column(row):
        return jnp.sum(jnp.where(t_row == t_col, row, jnp.zeros_like(row)), axis=1, keepdims=True)

    def x_out(which, d):
        there = (mine + d) % n_exp
        return send(
            rows_out.at[which, there], rows_in.at[which, d], x_send.at[which], x_recv.at[which], {"exp": there}
        )

    def x_all(which):
        ref = rows_in.at[which, pl.ds(1, n_exp - 1)]
        return send(ref, ref, x_send.at[which], x_recv.at[which], to_mate)

    def route(which, ids_ref, x_ref):
        ids = ids_ref[...]
        row0, row1 = ids[0:1, :], ids[1:2, :]
        e_row = lax.broadcasted_iota(jnp.int32, (n_exp, tokens), 0)
        named_row = jnp.where((e_row == row0) | (e_row == row1), 1.0, 0.0).astype(F32)
        after = jnp.where(t_row < t_col, 1.0, 0.0).astype(BF16)
        rank_row = jnp.dot(named_row.astype(BF16), after, preferred_element_type=F32)
        place_row = lax.broadcasted_iota(jnp.int32, (cap, tokens), 0).astype(F32)
        x = x_ref[...]
        for e in range(n_exp):
            chosen = jnp.where(place_row == rank_row[e : e + 1, :], named_row[e : e + 1, :], 0.0)
            rows_out[which, e] = jnp.dot(chosen.astype(BF16), x, preferred_element_type=F32).astype(BF16)
        for d in range(1, n_exp):
            x_out(which, d).start()
        rows_in[which, 0] = rows_out[which, mine]

    @pl.when(hub)
    def _():
        route(1, ids_in, x_in)

    def kv_relay(s, carry):
        origin = z - s

        @pl.when(origin >= 0)
        def _():
            slot = origin * 2 + core
            for copy in kv_wait(slot, kv_recv.at[slot]):
                copy.wait_recv()

            @pl.when(has_side(1))
            def _():
                for copy in kv_copies(origin, kv_send, to_side(1)):
                    copy.start()

            for copy in kv_copies(origin, kv_swap, to_mate):
                copy.start()

        return carry

    lax.fori_loop(1, n_z, kv_relay, 0)

    @pl.when(hub)
    def _():
        share_wide(1)

    ids = ids_in[...]
    probs = prob_in[...]
    id0, id1 = as_column(ids[0:1, :]), as_column(ids[1:2, :])
    e_col = lax.broadcasted_iota(jnp.int32, (tokens, n_exp), 1)
    named_col = jnp.where((e_col == id0) | (e_col == id1), 1.0, 0.0).astype(F32)
    before = jnp.where(t_col < t_row, 1.0, 0.0).astype(BF16)
    rank_col = jnp.dot(before, named_col.astype(BF16), preferred_element_type=F32)
    weight_col = jnp.where(e_col == id0, as_column(probs[0:1, :]), 0.0) + jnp.where(
        e_col == id1, as_column(probs[1:2, :]), 0.0
    )
    place_col = lax.broadcasted_iota(jnp.int32, (tokens, cap), 1).astype(F32)
    for e in range(n_exp):
        back = jnp.where(place_col == rank_col[:, e : e + 1], named_col[:, e : e + 1], 0.0)
        pick[e] = back.astype(BF16)
        gates[e] = weight_col[:, e : e + 1]

    def kv_from_mate(origin, carry):
        @pl.when(origin <= z)
        def _():
            slot = origin * 2 + other
            for copy in kv_wait(slot, kv_recv.at[slot]):
                copy.wait_recv()

        @pl.when(origin > z)
        def _():
            both = pl.ds(pl.multiple_of(origin * 2 * tokens, 2 * tokens), 2 * tokens)
            kv_buf[:, both] = jnp.zeros((2, 2 * tokens, kv_buf.shape[2]), BF16)
            seg_buf[pl.ds(origin * 2, 2)] = jnp.zeros((2, 1, tokens), jnp.int32)

        return carry

    lax.fori_loop(0, n_z, kv_from_mate, 0)
    for copy in local[3:]:
        copy.wait()

    own_segment = jnp.sum(
        jnp.where(t_row == t_col, jnp.broadcast_to(seg_buf[me], (tokens, tokens)), 0), axis=1, keepdims=True
    )
    source_segment = jnp.where(own_segment % 2 == 1, own_segment - 1, own_segment)
    for c in range(n_ctx):
        theirs = seg_buf[c]
        allowed = (t_col + c * tokens <= t_row + me * tokens) & (
            (theirs == own_segment) | (theirs == source_segment)
        )
        bias[:, c * tokens : (c + 1) * tokens] = jnp.where(allowed, 0.0, -1e30)

    def relay_wide(s, k):
        for side in (0, 1):
            origin = z - s if side else z + s

            @pl.when((origin >= 0) & (origin < n_z) & inner)
            def _():
                here = wide_piece(k, origin)
                wide_side(side, here, origin, k).wait_recv()

                @pl.when(takes(side))
                def _():
                    wide_side(side, here, origin, k).start()

                @pl.when(hub)
                def _():
                    wide_mate(here, origin, k).start()

    scale = HEAD_SIZE ** -0.5 * math.log2(math.e)

    def attend(g, carry):
        lanes = pl.ds(pl.multiple_of(g * HEAD_SIZE, HEAD_SIZE), HEAD_SIZE)

        def heads(i, inner_carry):
            for u in range(HEADS_AT_ONCE):
                head = g * group + i * HEADS_AT_ONCE + u
                at = pl.ds(pl.multiple_of(head * HEAD_SIZE, HEAD_SIZE), HEAD_SIZE)
                scores = lax.dot_general(
                    q_buf[:, at], kv_buf[0, :, lanes], (((1,), (1,)), ((), ())), preferred_element_type=F32
                )
                scores = scores * scale + bias[...]
                peak = jnp.max(scores, axis=1, keepdims=True)
                power = jnp.exp2(scores - peak)
                share = 1.0 / jnp.sum(power, axis=1, keepdims=True)
                mixed = jnp.dot(power.astype(BF16), kv_buf[1, :, lanes], preferred_element_type=F32)
                q_buf[:, at] = (mixed * share).astype(BF16)
            return inner_carry

        lax.fori_loop(0, group // HEADS_AT_ONCE, heads, 0)

        @pl.when((g == 1) & hub)
        def _():
            for j in range(2):
                x_to_hub(j).wait_recv()
            route(0, ids_peer, x_peer)

        for k in range(WIDE):
            @pl.when(g == min(k + 1, KEY_HEAD_COUNT - 1))
            def _():
                relay_wide(1, k)

        return carry

    lax.fori_loop(0, KEY_HEAD_COUNT, attend, 0)
    ctx_copy = pltpu.make_async_copy(q_buf, ctx_out, out_sem.at[0])
    ctx_copy.start()

    @pl.when(hub)
    def _():
        for which in (1, 0):
            x_all(which).wait_recv()
    for copy in local[:3]:
        copy.wait()

    def h_back(origin):
        return send(hidden.at[0, origin], hidden.at[1, origin], h_send.at[0], h_recv.at[0], to_peer)

    h_all = send(hidden.at[0], hidden.at[1], h_send.at[0], h_recv.at[0], to_peer)

    def hidden_of(origin):
        wide_all(origin, other, w_swapped.at[origin]).wait_recv()
        inputs = rows_in[...].reshape(2 * n_exp * cap, width)
        gate_w = weights[0, origin].reshape(-1, width)
        up_w = weights[1, origin].reshape(-1, width)
        gate = lax.dot_general(inputs, gate_w, (((1,), (1,)), ((), ())), preferred_element_type=F32)
        up = lax.dot_general(inputs, up_w, (((1,), (1,)), ((), ())), preferred_element_type=F32)
        units = (gate / (1.0 + jnp.exp(-gate)) * up).astype(BF16)
        hidden[0, origin] = units[: n_exp * cap]
        hidden[1, origin] = units[n_exp * cap :]
        h_back(origin).start()

    def pair_half(i):
        down_peer(i).wait_recv()
        per = COLUMN_BLOCKS // 2
        for side in (0, 1):
            @pl.when(has_side(side) & jnp.logical_not(peer_side(side)))
            def _():
                for c in range(per):
                    unit_side(side, pair, i * per + c).start()
        down_peer_mate(i).start()

    def far(t, carry):
        s = (t + 1) // 2
        origin = z + jnp.where(t % 2 == 1, -toward, toward) * s

        @pl.when(t == 2)
        def _():
            pair_half(0)

        @pl.when(t == jnp.where(z < n_z // 2, 2 * n_z - 1, 3))
        def _():
            pair_half(1)

        @pl.when((t % 2 == 1) & (s > 1))
        def _():
            for k in range(WIDE):
                relay_wide(s, k)

        @pl.when(hub & (origin >= 0) & (origin < n_z) & (t < 2 * n_z - 1))
        def _():
            hidden_of(origin)

        return carry

    lax.fori_loop(0, 2 * n_z, far, 0)

    @pl.when(client)
    def _():
        h_all.wait_recv()
    hidden_all[...] = jnp.concatenate([hidden[1, o] for o in range(n_z)], axis=1)
    own_unit = unit(pair, other)
    send(own_unit, own_unit, d_swap.at[0], d_swapped.at[0], to_mate).wait_recv()

    def r_out(d, cb):
        return send(
            result.at[d, :, block(cb)], returned.at[d - 1, :, block(cb)],
            r_send.at[0], r_recv.at[cb], {"exp": (mine + n_exp - d) % n_exp},
        )

    def r_block(cb):
        ref = returned.at[:, :, block(cb)]
        return send(ref, ref, r_send.at[0], r_recv.at[cb], to_mate)

    def mix_copy(cb):
        return pltpu.make_async_copy(mix_buf.at[:, block(cb)], mix_out.at[:, block(cb)], out_sem.at[1])

    def combine(cb):
        at = block(cb)
        mix = gates[mine] * jnp.dot(pick[mine], result[0, :, at], preferred_element_type=F32)
        r_block(cb).wait_recv()
        for d in range(1, n_exp):
            source = (mine + d) % n_exp
            mix += gates[source] * jnp.dot(pick[source], returned[d - 1, :, at], preferred_element_type=F32)
        mix_buf[:, at] = mix.astype(BF16)
        mix_copy(cb).start()

    def each_other(what):
        def one(s, carry):
            for side in (0, 1):
                q = pair - s if side else pair + s

                @pl.when((q >= 0) & (q < n_pair))
                def _():
                    what(side, q)

            return carry

        lax.fori_loop(1, n_pair, one, 0)

    def early_sends():
        @pl.when(has_side(1))
        def _():
            for copy in kv_wait(me, kv_send.at[z]):
                copy.wait_send()
        for copy in kv_wait(me, kv_swap.at[z]):
            copy.wait_send()

        def kv_sent(s, carry):
            origin = z - s

            @pl.when(origin >= 0)
            def _():
                @pl.when(has_side(1))
                def _():
                    for copy in kv_wait(origin * 2 + core, kv_send.at[origin]):
                        copy.wait_send()

                for copy in kv_wait(origin * 2 + core, kv_swap.at[origin]):
                    copy.wait_send()

            return carry

        lax.fori_loop(1, n_z, kv_sent, 0)

        @pl.when(client)
        def _():
            for j in range(2):
                x_to_hub(j).wait_send()

        @pl.when(hub)
        def _():
            for which in (0, 1):
                x_all(which).wait_send()
            h_all.wait_send()

        def wide_sent(origin, carry):
            for side in (0, 1):
                @pl.when(takes(side) & ((origin == z) | (inner & (origin < z if side else origin > z))))
                def _():
                    wide_all(origin, core, w_send.at[side, origin]).wait_send()

            @pl.when(hub)
            def _():
                wide_all(origin, core, w_send.at[2, origin]).wait_send()

            return carry

        lax.fori_loop(0, n_z, wide_sent, 0)
        d_all = weights.at[2, z, core]
        send(d_all, d_all, d_send.at[0], d_recv.at[0], to_mate).wait_send()
        swapped = unit(pair, core)
        send(swapped, swapped, d_swap.at[0], d_swapped.at[0], to_mate).wait_send()

    def down_block(cb, carry):
        @pl.when(cb < COLUMN_BLOCKS)
        def _():
            def pass_on(side, q):
                unit_side(side, q, cb).wait_recv()

                @pl.when(has_side(side))
                def _():
                    unit_side(side, q, cb).start()

                unit_mate(q, cb).start()

            each_other(pass_on)
            each_other(lambda side, q: unit_from_mate(q, cb).wait_recv())
            down_w = weights[2, :, :, :, block(cb)].reshape(-1, columns)
            out = jnp.dot(hidden_all[...], down_w, preferred_element_type=F32)
            result[:, :, block(cb)] = out.astype(BF16).reshape(n_exp, cap, columns)
            for d in range(1, n_exp):
                r_out(d, cb).start()

        @pl.when(cb >= LAG)
        def _():
            combine(cb - LAG)

        @pl.when(cb == LAG)
        def _():
            early_sends()

        return carry

    lax.fori_loop(0, COLUMN_BLOCKS + LAG, down_block, 0)

    for side in (0, 1):
        @pl.when(has_side(side) & jnp.logical_not(peer_side(side)))
        def _():
            ref = unit(pair, core)
            send(ref, ref, u_send.at[pair], u_send.at[pair], to_mate).wait_send()

    def units_sent(side, q):
        ref = unit(q, core)

        @pl.when(has_side(side))
        def _():
            send(ref, ref, u_send.at[q], u_send.at[q], to_mate).wait_send()

        send(ref, ref, u_swap.at[q], u_swap.at[q], to_mate).wait_send()

    each_other(units_sent)
    send(returned, returned, r_send.at[0], r_send.at[0], to_mate).wait_send()
    pltpu.make_async_copy(mix_buf, mix_out, out_sem.at[1]).wait()
    ctx_copy.wait()


def on_device(
    n_ctx, n_exp,
    queries, key_head_vectors, value_head_vectors, segment_ids,
    normed, expert_ids, gate_probs, gate_weight, up_weight, down_weight,
):
    tokens, q_width = queries.shape[1:]
    kv_width = key_head_vectors.shape[2]
    width = normed.shape[2]
    hidden = gate_weight.shape[1]
    most = tokens * expert_ids.shape[2] * 5 // (4 * n_exp)
    cap = -(-most // 16) * 16
    span = n_ctx * tokens
    n_z = n_ctx // 2
    dma = pltpu.SemaphoreType.DMA
    hbm = pl.BlockSpec(memory_space=pl.ANY)
    vmem = pl.BlockSpec(memory_space=pltpu.VMEM)
    context, mixture = pl.pallas_call(
        functools.partial(kernel, n_ctx, n_exp, cap),
        out_shape=(
            jax.ShapeDtypeStruct((tokens, q_width), BF16),
            jax.ShapeDtypeStruct((tokens, width), BF16),
        ),
        in_specs=[hbm, hbm, hbm, vmem, vmem, vmem, vmem, hbm, hbm, hbm],
        out_specs=(hbm, hbm),
        scratch_shapes=[
            pltpu.VMEM((tokens, q_width), BF16),
            pltpu.VMEM((2, span, kv_width), BF16),
            pltpu.VMEM((n_ctx, 1, tokens), jnp.int32),
            pltpu.VMEM((tokens, span), F32),
            pltpu.VMEM((3, n_z, 2, hidden, width), BF16),
            pltpu.VMEM((tokens, width), BF16),
            pltpu.VMEM((expert_ids.shape[2], tokens), jnp.int32),
            pltpu.VMEM((2, n_exp, cap, width), BF16),
            pltpu.VMEM((2, n_exp, cap, width), BF16),
            pltpu.VMEM((2, n_z, n_exp * cap, 2 * hidden), BF16),
            pltpu.VMEM((n_exp * cap, n_ctx * hidden), BF16),
            pltpu.VMEM((n_exp, cap, width), BF16),
            pltpu.VMEM((n_exp - 1, cap, width), BF16),
            pltpu.VMEM((n_exp, tokens, cap), BF16),
            pltpu.VMEM((n_exp, tokens, 1), F32),
            pltpu.VMEM((tokens, width), BF16),
            dma((7,)),
            dma((n_z, 2)),
            dma((n_z, 2)),
            dma((n_ctx, 2)),
            dma((3, n_z)),
            dma((n_z, WIDE)),
            dma((n_z,)),
            dma((1,)),
            dma((2,)),
            dma((1,)),
            dma((1,)),
            dma((n_z // 2,)),
            dma((n_z // 2, COLUMN_BLOCKS)),
            dma((n_z // 2,)),
            dma((n_z // 2, COLUMN_BLOCKS)),
            dma((2,)),
            dma((2,)),
            dma((2,)),
            dma((2,)),
            dma((1,)),
            dma((1,)),
            dma((1,)),
            dma((COLUMN_BLOCKS,)),
            dma((2,)),
        ],
        compiler_params=pltpu.CompilerParams(
            collective_id=0, has_side_effects=True, vmem_limit_bytes=60 * 1024 * 1024
        ),
        name="layer",
    )(
        queries[0], key_head_vectors[0], value_head_vectors[0], segment_ids,
        normed[0], expert_ids[0].T, gate_probs[0].T, gate_weight[0], up_weight[0], down_weight[0],
    )
    return context[None], mixture[None]


def solution(mesh):
    rows = P("exp", "ctx", None)
    in_specs = (rows, rows, rows, P("exp", "ctx"), rows, rows, rows, rows, rows, rows)
    return jax.shard_map(
        functools.partial(on_device, mesh.shape["ctx"], mesh.shape["exp"]),
        mesh=mesh, in_specs=in_specs, out_specs=(rows, rows), check_vma=False,
    )
```

```python
import functools
import math

import jax
import jax.numpy as jnp
from jax import lax
from jax.experimental import pallas as pl
from jax.experimental.pallas import tpu as pltpu
from jax.sharding import PartitionSpec as P

KEY_HEAD_COUNT = 4
HEAD_SIZE = 128
COLUMN_BLOCKS = 16
HEADS_AT_ONCE = 4
HALVES = 2
WIDE = 2 * HALVES
LAG = 2
MESH = pl.DeviceIdType.MESH
F32 = jnp.float32
BF16 = jnp.bfloat16


def kernel(
    n_ctx, n_exp, cap,
    q_hbm, k_hbm, v_hbm, seg_in, x_in, ids_in, prob_in, gate_hbm, up_hbm, down_hbm,
    ctx_out, mix_out,
    q_buf, kv_buf, seg_buf, bias, weights, x_peer, ids_peer, rows_out, rows_in,
    hidden, gated, hidden_all, result, returned, pick, gates, mix_buf,
    local_sem, kv_send, kv_swap, kv_recv, w_send, w_recv, w_swapped,
    d_send, d_recv, d_swap, d_swapped, u_send, u_recv, u_swap, u_swapped,
    t_send, t_recv, x_send, x_recv, h_send, h_recv, r_send, r_recv, out_sem,
):
    me = lax.axis_index("ctx")
    mine = lax.axis_index("exp")
    n_z = n_ctx // 2
    n_pair = n_z // 2
    z, core = me // 2, me % 2
    other = 1 - core
    mate = me + 1 - 2 * core
    toward = 1 - 2 * (z % 2)
    peer = z + toward
    pair = z // 2
    hub = jnp.where(z < n_z // 2, z % 2 == 1, z % 2 == 0)
    client = jnp.logical_not(hub)
    inner = (z > 0) & (z < n_z - 1)
    tokens, width = x_in.shape
    group = q_buf.shape[1] // (KEY_HEAD_COUNT * HEAD_SIZE)
    columns = width // COLUMN_BLOCKS
    half = width // HALVES

    def send(src, dst, send_sem, recv_sem, where):
        return pltpu.make_async_remote_copy(
            src_ref=src, dst_ref=dst, send_sem=send_sem, recv_sem=recv_sem,
            device_id=where, device_id_type=MESH,
        )

    to_mate = {"ctx": mate}
    to_peer = {"ctx": peer * 2 + core}

    def to_side(side):
        return {"ctx": me + 2 if side else me - 2}

    def block(cb):
        return pl.ds(pl.multiple_of(cb * columns, columns), columns)

    def has_side(side):
        return z + 1 < n_z if side else z > 0

    def takes(side):
        return z + 1 < n_z - 1 if side else z > 1

    def peer_side(side):
        return z % 2 == 1 - side

    barrier = pltpu.get_barrier_semaphore()
    for side in (0, 1):
        @pl.when(has_side(side))
        def _():
            pl.semaphore_signal(barrier, inc=1, device_id=to_side(side), device_id_type=MESH)
    pl.semaphore_signal(barrier, inc=1, device_id=to_mate, device_id_type=MESH)
    for d in range(1, n_exp):
        pl.semaphore_signal(barrier, inc=1, device_id={"exp": (mine + d) % n_exp}, device_id_type=MESH)
    pl.semaphore_wait(barrier, n_exp + jnp.where(inner, 2, 1))

    def kv_rows(slot):
        return kv_buf.at[:, pl.ds(pl.multiple_of(slot * tokens, tokens), tokens)]

    def kv_copies(origin, sem, where, own=False):
        slot = origin * 2 + core
        rows = pl.ds(pl.multiple_of(slot * tokens, tokens), tokens)
        if own:
            pairs = [(k_hbm, kv_buf.at[0, rows], 0), (v_hbm, kv_buf.at[1, rows], 0), (seg_in, seg_buf.at[slot], 1)]
        else:
            pairs = [(kv_rows(slot), kv_rows(slot), 0), (seg_buf.at[slot], seg_buf.at[slot], 1)]
        return [send(src, dst, sem.at[origin, j], kv_recv.at[slot, j], where) for src, dst, j in pairs]

    def kv_wait(slot, sems):
        refs = (kv_rows(slot), seg_buf.at[slot])
        return [send(refs[j], refs[j], sems.at[j], sems.at[j], to_mate) for j in range(2)]

    @pl.when(has_side(1))
    def _():
        for copy in kv_copies(z, kv_send, to_side(1), own=True):
            copy.start()
    for copy in kv_copies(z, kv_swap, to_mate, own=True):
        copy.start()

    def wide_own(k):
        return (gate_hbm, up_hbm)[k // HALVES].at[:, pl.ds(k % HALVES * half, half)]

    def wide_piece(k, origin):
        return weights.at[k // HALVES, origin, core, :, pl.ds(k % HALVES * half, half)]

    def wide_side(side, src, origin, k):
        return send(src, wide_piece(k, origin), w_send.at[side, origin], w_recv.at[origin, k], to_side(side))

    def wide_mate(src, origin, k):
        return send(src, wide_piece(k, origin), w_send.at[2, origin], w_swapped.at[origin, k // HALVES], to_mate)

    def wide_all(origin, which, sem):
        ref = weights.at[pl.ds(0, 2), origin, which]
        return send(ref, ref, sem, sem, to_mate)

    def wide_from_mate(origin, w):
        ref = weights.at[w, origin, other]
        return send(ref, ref, w_send.at[2, origin], w_swapped.at[origin, w], to_mate)

    def share_wide(side):
        @pl.when(takes(side))
        def _():
            for k in range(WIDE):
                wide_side(side, wide_own(k), z, k).start()

    def x_to_hub(j):
        src, dst = ((ids_in, ids_peer), (x_in, x_peer))[j]
        return send(src, dst, t_send.at[j], t_recv.at[j], to_peer)

    @pl.when(client)
    def _():
        for j in range(2):
            x_to_hub(j).start()
        share_wide(1)
    share_wide(0)

    d_half = width // 2

    def down_own(i):
        cols = pl.ds(pl.multiple_of(i * d_half, d_half), d_half)
        return send(
            down_hbm.at[:, cols], weights.at[2, z, core, :, cols], d_send.at[0], d_recv.at[i], to_peer
        )

    def down_peer(i):
        cols = pl.ds(pl.multiple_of(i * d_half, d_half), d_half)
        here = weights.at[2, peer, core, :, cols]
        return send(here, here, d_swap.at[0], d_recv.at[i], to_mate)

    def down_own_mate():
        return send(down_hbm, weights.at[2, z, core], d_swap.at[0], d_swapped.at[0], to_mate)

    def down_peer_mate(i):
        cols = pl.ds(pl.multiple_of(i * d_half, d_half), d_half)
        here = weights.at[2, peer, core, :, cols]
        return send(here, here, d_swap.at[0], d_swapped.at[0], to_mate)

    def unit(q, which, cols=slice(None)):
        return weights.at[2, pl.ds(q * 2, 2), which, :, cols]

    def unit_side(side, q, cb):
        ref = unit(q, core, block(cb))
        return send(ref, ref, u_send.at[q], u_recv.at[q, cb], to_side(side))

    def unit_mate(q, cb):
        ref = unit(q, core, block(cb))
        return send(ref, ref, u_swap.at[q], u_swapped.at[q, cb], to_mate)

    def unit_from_mate(q, cb):
        ref = unit(q, other, block(cb))
        return send(ref, ref, u_swap.at[q], u_swapped.at[q, cb], to_mate)

    for i in range(2):
        down_own(i).start()

    @pl.when(hub)
    def _():
        for k in range(WIDE):
            wide_mate(wide_own(k), z, k).start()
    down_own_mate().start()

    local = [
        pltpu.make_async_copy(w, weights.at[k, z, core], local_sem.at[k])
        for k, w in enumerate((gate_hbm, up_hbm, down_hbm))
    ]
    my_rows = pl.ds(pl.multiple_of(me * tokens, tokens), tokens)
    local += [
        pltpu.make_async_copy(k_hbm, kv_buf.at[0, my_rows], local_sem.at[3]),
        pltpu.make_async_copy(v_hbm, kv_buf.at[1, my_rows], local_sem.at[4]),
        pltpu.make_async_copy(seg_in, seg_buf.at[me], local_sem.at[5]),
        pltpu.make_async_copy(q_hbm, q_buf, local_sem.at[6]),
    ]
    for copy in local:
        copy.start()

    t_row = lax.broadcasted_iota(jnp.int32, (tokens, tokens), 0)
    t_col = lax.broadcasted_iota(jnp.int32, (tokens, tokens), 1)

    def as_column(row):
        return jnp.sum(jnp.where(t_row == t_col, row, jnp.zeros_like(row)), axis=1, keepdims=True)

    def x_out(which, d):
        there = (mine + d) % n_exp
        return send(
            rows_out.at[which, there], rows_in.at[which, d], x_send.at[which], x_recv.at[which], {"exp": there}
        )

    def x_all(which):
        ref = rows_in.at[which, pl.ds(1, n_exp - 1)]
        return send(ref, ref, x_send.at[which], x_recv.at[which], to_mate)

    def route(which, ids_ref, x_ref):
        ids = ids_ref[...]
        row0, row1 = ids[0:1, :], ids[1:2, :]
        e_row = lax.broadcasted_iota(jnp.int32, (n_exp, tokens), 0)
        named_row = jnp.where((e_row == row0) | (e_row == row1), 1.0, 0.0).astype(F32)
        after = jnp.where(t_row < t_col, 1.0, 0.0).astype(BF16)
        rank_row = jnp.dot(named_row.astype(BF16), after, preferred_element_type=F32)
        place_row = lax.broadcasted_iota(jnp.int32, (cap, tokens), 0).astype(F32)
        x = x_ref[...]
        for e in range(n_exp):
            chosen = jnp.where(place_row == rank_row[e : e + 1, :], named_row[e : e + 1, :], 0.0)
            rows_out[which, e] = jnp.dot(chosen.astype(BF16), x, preferred_element_type=F32).astype(BF16)
        for d in range(1, n_exp):
            x_out(which, d).start()
        rows_in[which, 0] = rows_out[which, mine]

    @pl.when(hub)
    def _():
        route(1, ids_in, x_in)

    def kv_relay(s, carry):
        origin = z - s

        @pl.when(origin >= 0)
        def _():
            slot = origin * 2 + core
            for copy in kv_wait(slot, kv_recv.at[slot]):
                copy.wait_recv()

            @pl.when(has_side(1))
            def _():
                for copy in kv_copies(origin, kv_send, to_side(1)):
                    copy.start()

            for copy in kv_copies(origin, kv_swap, to_mate):
                copy.start()

        return carry

    lax.fori_loop(1, n_z, kv_relay, 0)

    @pl.when(hub)
    def _():
        share_wide(1)

    ids = ids_in[...]
    probs = prob_in[...]
    id0, id1 = as_column(ids[0:1, :]), as_column(ids[1:2, :])
    e_col = lax.broadcasted_iota(jnp.int32, (tokens, n_exp), 1)
    named_col = jnp.where((e_col == id0) | (e_col == id1), 1.0, 0.0).astype(F32)
    before = jnp.where(t_col < t_row, 1.0, 0.0).astype(BF16)
    rank_col = jnp.dot(before, named_col.astype(BF16), preferred_element_type=F32)
    weight_col = jnp.where(e_col == id0, as_column(probs[0:1, :]), 0.0) + jnp.where(
        e_col == id1, as_column(probs[1:2, :]), 0.0
    )
    place_col = lax.broadcasted_iota(jnp.int32, (tokens, cap), 1).astype(F32)
    for e in range(n_exp):
        back = jnp.where(place_col == rank_col[:, e : e + 1], named_col[:, e : e + 1], 0.0)
        pick[e] = back.astype(BF16)
        gates[e] = weight_col[:, e : e + 1]

    def kv_from_mate(origin, carry):
        @pl.when(origin <= z)
        def _():
            slot = origin * 2 + other
            for copy in kv_wait(slot, kv_recv.at[slot]):
                copy.wait_recv()

        @pl.when(origin > z)
        def _():
            both = pl.ds(pl.multiple_of(origin * 2 * tokens, 2 * tokens), 2 * tokens)
            kv_buf[:, both] = jnp.zeros((2, 2 * tokens, kv_buf.shape[2]), BF16)
            seg_buf[pl.ds(origin * 2, 2)] = jnp.zeros((2, 1, tokens), jnp.int32)

        return carry

    lax.fori_loop(0, n_z, kv_from_mate, 0)
    for copy in local[3:]:
        copy.wait()

    own_segment = jnp.sum(
        jnp.where(t_row == t_col, jnp.broadcast_to(seg_buf[me], (tokens, tokens)), 0), axis=1, keepdims=True
    )
    source_segment = jnp.where(own_segment % 2 == 1, own_segment - 1, own_segment)
    for c in range(n_ctx):
        theirs = seg_buf[c]
        allowed = (t_col + c * tokens <= t_row + me * tokens) & (
            (theirs == own_segment) | (theirs == source_segment)
        )
        bias[:, c * tokens : (c + 1) * tokens] = jnp.where(allowed, 0.0, -1e30)

    def relay_wide(s, k):
        for side in (0, 1):
            origin = z - s if side else z + s

            @pl.when((origin >= 0) & (origin < n_z) & inner)
            def _():
                here = wide_piece(k, origin)
                wide_side(side, here, origin, k).wait_recv()

                @pl.when(takes(side))
                def _():
                    wide_side(side, here, origin, k).start()

                @pl.when(hub)
                def _():
                    wide_mate(here, origin, k).start()

    scale = HEAD_SIZE ** -0.5 * math.log2(math.e)

    def attend(g, carry):
        lanes = pl.ds(pl.multiple_of(g * HEAD_SIZE, HEAD_SIZE), HEAD_SIZE)

        def heads(i, inner_carry):
            for u in range(HEADS_AT_ONCE):
                head = g * group + i * HEADS_AT_ONCE + u
                at = pl.ds(pl.multiple_of(head * HEAD_SIZE, HEAD_SIZE), HEAD_SIZE)
                scores = lax.dot_general(
                    q_buf[:, at], kv_buf[0, :, lanes], (((1,), (1,)), ((), ())), preferred_element_type=F32
                )
                scores = scores * scale + bias[...]
                peak = jnp.max(scores, axis=1, keepdims=True)
                power = jnp.exp2(scores - peak)
                share = 1.0 / jnp.sum(power, axis=1, keepdims=True)
                mixed = jnp.dot(power.astype(BF16), kv_buf[1, :, lanes], preferred_element_type=F32)
                q_buf[:, at] = (mixed * share).astype(BF16)
            return inner_carry

        lax.fori_loop(0, group // HEADS_AT_ONCE, heads, 0)

        @pl.when((g == 1) & hub)
        def _():
            for j in range(2):
                x_to_hub(j).wait_recv()
            route(0, ids_peer, x_peer)

        for k in range(WIDE):
            @pl.when(g == min(k + 1, KEY_HEAD_COUNT - 1))
            def _():
                relay_wide(1, k)

        return carry

    lax.fori_loop(0, KEY_HEAD_COUNT, attend, 0)
    ctx_copy = pltpu.make_async_copy(q_buf, ctx_out, out_sem.at[0])
    ctx_copy.start()

    @pl.when(hub)
    def _():
        for which in (1, 0):
            x_all(which).wait_recv()
    for copy in local[:3]:
        copy.wait()

    def h_back(origin):
        return send(hidden.at[0, origin], hidden.at[1, origin], h_send.at[0], h_recv.at[0], to_peer)

    h_all = send(hidden.at[0], hidden.at[1], h_send.at[0], h_recv.at[0], to_peer)

    def product(origin, w):
        wide_from_mate(origin, w).wait_recv()
        return lax.dot_general(
            rows_in[...].reshape(2 * n_exp * cap, width), weights[w, origin].reshape(-1, width),
            (((1,), (1,)), ((), ())), preferred_element_type=F32,
        )

    def gate_of(origin):
        gate = product(origin, 0)
        gated[...] = gate / (1.0 + jnp.exp(-gate))

    def hidden_of(origin):
        units = (gated[...] * product(origin, 1)).astype(BF16)
        hidden[0, origin] = units[: n_exp * cap]
        hidden[1, origin] = units[n_exp * cap :]
        h_back(origin).start()

    def pair_half(i):
        down_peer(i).wait_recv()
        per = COLUMN_BLOCKS // 2
        for side in (0, 1):
            @pl.when(has_side(side) & jnp.logical_not(peer_side(side)))
            def _():
                for c in range(per):
                    unit_side(side, pair, i * per + c).start()
        down_peer_mate(i).start()

    def each_other(what):
        def one(s, carry):
            for side in (0, 1):
                q = pair - s if side else pair + s

                @pl.when((q >= 0) & (q < n_pair))
                def _():
                    what(side, q)

            return carry

        lax.fori_loop(1, n_pair, one, 0)

    def pass_units(cb):
        def one(side, q):
            unit_side(side, q, cb).wait_recv()

            @pl.when(has_side(side))
            def _():
                unit_side(side, q, cb).start()

            unit_mate(q, cb).start()

        each_other(one)

    early = 3 if n_pair == 2 else 0
    ahead = hub & (z < n_z // 2) & (early > 0)

    def far(t, carry):
        s = (t + 1) // 2
        origin = z + jnp.where(t % 2 == 1, -toward, toward) * s

        @pl.when(t == 2)
        def _():
            pair_half(0)

        @pl.when(t == jnp.where(z < n_z // 2, 2 * n_z - 1, 3))
        def _():
            pair_half(1)

        here = hub & (origin >= 0) & (origin < n_z) & (t < 2 * n_z - 1)
        for w, what in enumerate((gate_of, hidden_of)):
            @pl.when(ahead & (t == 3))
            def _():
                pass_units(w)

            @pl.when((t % 2 == 1) & (s > 1))
            def _():
                for k in range(w * HALVES, (w + 1) * HALVES):
                    relay_wide(s, k)

            @pl.when(here)
            def _():
                what(origin)

        return carry

    lax.fori_loop(0, 2 * n_z, far, 0)

    @pl.when(ahead)
    def _():
        pass_units(2)

    @pl.when(jnp.logical_not(ahead))
    def _():
        pass_units(0)

    @pl.when(client)
    def _():
        h_all.wait_recv()
    hidden_all[...] = jnp.concatenate([hidden[1, o] for o in range(n_z)], axis=1)
    own_unit = unit(pair, other)
    send(own_unit, own_unit, d_swap.at[0], d_swapped.at[0], to_mate).wait_recv()

    def r_out(d, cb):
        return send(
            result.at[d, :, block(cb)], returned.at[d - 1, :, block(cb)],
            r_send.at[0], r_recv.at[cb], {"exp": (mine + n_exp - d) % n_exp},
        )

    def r_block(cb):
        ref = returned.at[:, :, block(cb)]
        return send(ref, ref, r_send.at[0], r_recv.at[cb], to_mate)

    def mix_copy(cb):
        return pltpu.make_async_copy(mix_buf.at[:, block(cb)], mix_out.at[:, block(cb)], out_sem.at[1])

    def combine(cb):
        at = block(cb)
        mix = gates[mine] * jnp.dot(pick[mine], result[0, :, at], preferred_element_type=F32)
        r_block(cb).wait_recv()
        for d in range(1, n_exp):
            source = (mine + d) % n_exp
            mix += gates[source] * jnp.dot(pick[source], returned[d - 1, :, at], preferred_element_type=F32)
        mix_buf[:, at] = mix.astype(BF16)
        mix_copy(cb).start()

    def early_sends():
        @pl.when(has_side(1))
        def _():
            for copy in kv_wait(me, kv_send.at[z]):
                copy.wait_send()
        for copy in kv_wait(me, kv_swap.at[z]):
            copy.wait_send()

        def kv_sent(s, carry):
            origin = z - s

            @pl.when(origin >= 0)
            def _():
                @pl.when(has_side(1))
                def _():
                    for copy in kv_wait(origin * 2 + core, kv_send.at[origin]):
                        copy.wait_send()

                for copy in kv_wait(origin * 2 + core, kv_swap.at[origin]):
                    copy.wait_send()

            return carry

        lax.fori_loop(1, n_z, kv_sent, 0)

        @pl.when(client)
        def _():
            for j in range(2):
                x_to_hub(j).wait_send()

        @pl.when(hub)
        def _():
            for which in (0, 1):
                x_all(which).wait_send()
            h_all.wait_send()

        def wide_sent(origin, carry):
            for side in (0, 1):
                @pl.when(takes(side) & ((origin == z) | (inner & (origin < z if side else origin > z))))
                def _():
                    wide_all(origin, core, w_send.at[side, origin]).wait_send()

            @pl.when(hub)
            def _():
                wide_all(origin, core, w_send.at[2, origin]).wait_send()

            return carry

        lax.fori_loop(0, n_z, wide_sent, 0)
        d_all = weights.at[2, z, core]
        send(d_all, d_all, d_send.at[0], d_recv.at[0], to_mate).wait_send()
        swapped = unit(pair, core)
        send(swapped, swapped, d_swap.at[0], d_swapped.at[0], to_mate).wait_send()

    def down_block(cb, carry):
        @pl.when(cb < COLUMN_BLOCKS)
        def _():
            each_other(lambda side, q: unit_from_mate(q, cb).wait_recv())
            down_w = weights[2, :, :, :, block(cb)].reshape(-1, columns)
            out = jnp.dot(hidden_all[...], down_w, preferred_element_type=F32)
            result[:, :, block(cb)] = out.astype(BF16).reshape(n_exp, cap, columns)
            for d in range(1, n_exp):
                r_out(d, cb).start()

        @pl.when((cb + 1 >= jnp.where(ahead, early, 1)) & (cb < COLUMN_BLOCKS - 1))
        def _():
            pass_units(cb + 1)

        @pl.when(cb >= LAG)
        def _():
            combine(cb - LAG)

        @pl.when(cb == LAG)
        def _():
            early_sends()

        return carry

    lax.fori_loop(0, COLUMN_BLOCKS + LAG, down_block, 0)

    for side in (0, 1):
        @pl.when(has_side(side) & jnp.logical_not(peer_side(side)))
        def _():
            ref = unit(pair, core)
            send(ref, ref, u_send.at[pair], u_send.at[pair], to_mate).wait_send()

    def units_sent(side, q):
        ref = unit(q, core)

        @pl.when(has_side(side))
        def _():
            send(ref, ref, u_send.at[q], u_send.at[q], to_mate).wait_send()

        send(ref, ref, u_swap.at[q], u_swap.at[q], to_mate).wait_send()

    each_other(units_sent)
    send(returned, returned, r_send.at[0], r_send.at[0], to_mate).wait_send()
    pltpu.make_async_copy(mix_buf, mix_out, out_sem.at[1]).wait()
    ctx_copy.wait()


def on_device(
    n_ctx, n_exp,
    queries, key_head_vectors, value_head_vectors, segment_ids,
    normed, expert_ids, gate_probs, gate_weight, up_weight, down_weight,
):
    tokens, q_width = queries.shape[1:]
    kv_width = key_head_vectors.shape[2]
    width = normed.shape[2]
    hidden = gate_weight.shape[1]
    most = tokens * expert_ids.shape[2] * 5 // (4 * n_exp)
    cap = -(-most // 16) * 16
    span = n_ctx * tokens
    n_z = n_ctx // 2
    dma = pltpu.SemaphoreType.DMA
    hbm = pl.BlockSpec(memory_space=pl.ANY)
    vmem = pl.BlockSpec(memory_space=pltpu.VMEM)
    context, mixture = pl.pallas_call(
        functools.partial(kernel, n_ctx, n_exp, cap),
        out_shape=(
            jax.ShapeDtypeStruct((tokens, q_width), BF16),
            jax.ShapeDtypeStruct((tokens, width), BF16),
        ),
        in_specs=[hbm, hbm, hbm, vmem, vmem, vmem, vmem, hbm, hbm, hbm],
        out_specs=(hbm, hbm),
        scratch_shapes=[
            pltpu.VMEM((tokens, q_width), BF16),
            pltpu.VMEM((2, span, kv_width), BF16),
            pltpu.VMEM((n_ctx, 1, tokens), jnp.int32),
            pltpu.VMEM((tokens, span), F32),
            pltpu.VMEM((3, n_z, 2, hidden, width), BF16),
            pltpu.VMEM((tokens, width), BF16),
            pltpu.VMEM((expert_ids.shape[2], tokens), jnp.int32),
            pltpu.VMEM((2, n_exp, cap, width), BF16),
            pltpu.VMEM((2, n_exp, cap, width), BF16),
            pltpu.VMEM((2, n_z, n_exp * cap, 2 * hidden), BF16),
            pltpu.VMEM((2 * n_exp * cap, 2 * hidden), F32),
            pltpu.VMEM((n_exp * cap, n_ctx * hidden), BF16),
            pltpu.VMEM((n_exp, cap, width), BF16),
            pltpu.VMEM((n_exp - 1, cap, width), BF16),
            pltpu.VMEM((n_exp, tokens, cap), BF16),
            pltpu.VMEM((n_exp, tokens, 1), F32),
            pltpu.VMEM((tokens, width), BF16),
            dma((7,)),
            dma((n_z, 2)),
            dma((n_z, 2)),
            dma((n_ctx, 2)),
            dma((3, n_z)),
            dma((n_z, WIDE)),
            dma((n_z, 2)),
            dma((1,)),
            dma((2,)),
            dma((1,)),
            dma((1,)),
            dma((n_z // 2,)),
            dma((n_z // 2, COLUMN_BLOCKS)),
            dma((n_z // 2,)),
            dma((n_z // 2, COLUMN_BLOCKS)),
            dma((2,)),
            dma((2,)),
            dma((2,)),
            dma((2,)),
            dma((1,)),
            dma((1,)),
            dma((1,)),
            dma((COLUMN_BLOCKS,)),
            dma((2,)),
        ],
        compiler_params=pltpu.CompilerParams(
            collective_id=0, has_side_effects=True, vmem_limit_bytes=60 * 1024 * 1024
        ),
        name="layer",
    )(
        queries[0], key_head_vectors[0], value_head_vectors[0], segment_ids,
        normed[0], expert_ids[0].T, gate_probs[0].T, gate_weight[0], up_weight[0], down_weight[0],
    )
    return context[None], mixture[None]


def solution(mesh):
    rows = P("exp", "ctx", None)
    in_specs = (rows, rows, rows, P("exp", "ctx"), rows, rows, rows, rows, rows, rows)
    return jax.shard_map(
        functools.partial(on_device, mesh.shape["ctx"], mesh.shape["exp"]),
        mesh=mesh, in_specs=in_specs, out_specs=(rows, rows), check_vma=False,
    )
```

```python
import functools
import math

import jax
import jax.numpy as jnp
from jax import lax
from jax.experimental import pallas as pl
from jax.experimental.pallas import tpu as pltpu
from jax.sharding import PartitionSpec as P

KEY_HEAD_COUNT = 4
HEAD_SIZE = 128
COLUMN_BLOCKS = 16
HEADS_AT_ONCE = 4
HALVES = 2
WIDE = 2 * HALVES
LAG = 2
MESH = pl.DeviceIdType.MESH
F32 = jnp.float32
BF16 = jnp.bfloat16


def kernel(
    n_ctx, n_exp, cap,
    q_hbm, k_hbm, v_hbm, seg_in, x_in, ids_in, prob_in, gate_hbm, up_hbm, down_hbm,
    ctx_out, mix_out,
    q_buf, kv_buf, seg_buf, bias, weights, x_peer, ids_peer, rows_out, rows_in,
    hidden, gated, hidden_all, result, returned, pick, gates, mix_buf,
    local_sem, kv_send, kv_swap, kv_recv, w_send, w_recv, w_swapped,
    d_send, d_recv, d_swap, d_swapped, u_send, u_recv, u_swap, u_swapped,
    t_send, t_recv, x_send, x_recv, h_send, h_recv, r_send, r_recv, out_sem,
):
    me = lax.axis_index("ctx")
    mine = lax.axis_index("exp")
    n_z = n_ctx // 2
    n_pair = n_z // 2
    z, core = me // 2, me % 2
    other = 1 - core
    mate = me + 1 - 2 * core
    toward = 1 - 2 * (z % 2)
    peer = z + toward
    pair = z // 2
    hub = jnp.where(z < n_z // 2, z % 2 == 1, z % 2 == 0)
    client = jnp.logical_not(hub)
    inner = (z > 0) & (z < n_z - 1)
    tokens, width = x_in.shape
    group = q_buf.shape[1] // (KEY_HEAD_COUNT * HEAD_SIZE)
    columns = width // COLUMN_BLOCKS
    half = width // HALVES

    def send(src, dst, send_sem, recv_sem, where):
        return pltpu.make_async_remote_copy(
            src_ref=src, dst_ref=dst, send_sem=send_sem, recv_sem=recv_sem,
            device_id=where, device_id_type=MESH,
        )

    to_mate = {"ctx": mate}
    to_peer = {"ctx": peer * 2 + core}

    def to_side(side):
        return {"ctx": me + 2 if side else me - 2}

    def block(cb):
        return pl.ds(pl.multiple_of(cb * columns, columns), columns)

    def has_side(side):
        return z + 1 < n_z if side else z > 0

    def takes(side):
        return z + 1 < n_z - 1 if side else z > 1

    def peer_side(side):
        return z % 2 == 1 - side

    barrier = pltpu.get_barrier_semaphore()
    for side in (0, 1):
        @pl.when(has_side(side))
        def _():
            pl.semaphore_signal(barrier, inc=1, device_id=to_side(side), device_id_type=MESH)
    pl.semaphore_signal(barrier, inc=1, device_id=to_mate, device_id_type=MESH)
    for d in range(1, n_exp):
        pl.semaphore_signal(barrier, inc=1, device_id={"exp": (mine + d) % n_exp}, device_id_type=MESH)
    pl.semaphore_wait(barrier, n_exp + jnp.where(inner, 2, 1))

    def kv_rows(slot):
        return kv_buf.at[:, pl.ds(pl.multiple_of(slot * tokens, tokens), tokens)]

    def kv_copies(origin, sem, where, own=False):
        slot = origin * 2 + core
        rows = pl.ds(pl.multiple_of(slot * tokens, tokens), tokens)
        if own:
            pairs = [(k_hbm, kv_buf.at[0, rows], 0), (v_hbm, kv_buf.at[1, rows], 0), (seg_in, seg_buf.at[slot], 1)]
        else:
            pairs = [(kv_rows(slot), kv_rows(slot), 0), (seg_buf.at[slot], seg_buf.at[slot], 1)]
        return [send(src, dst, sem.at[origin, j], kv_recv.at[slot, j], where) for src, dst, j in pairs]

    def kv_wait(slot, sems):
        refs = (kv_rows(slot), seg_buf.at[slot])
        return [send(refs[j], refs[j], sems.at[j], sems.at[j], to_mate) for j in range(2)]

    @pl.when(has_side(1))
    def _():
        for copy in kv_copies(z, kv_send, to_side(1), own=True):
            copy.start()
    for copy in kv_copies(z, kv_swap, to_mate, own=True):
        copy.start()

    def wide_own(k):
        return (gate_hbm, up_hbm)[k // HALVES].at[:, pl.ds(k % HALVES * half, half)]

    def wide_piece(k, origin):
        return weights.at[k // HALVES, origin, core, :, pl.ds(k % HALVES * half, half)]

    def wide_side(side, src, origin, k):
        return send(src, wide_piece(k, origin), w_send.at[side, origin], w_recv.at[origin, k], to_side(side))

    def wide_mate(src, origin, k):
        return send(src, wide_piece(k, origin), w_send.at[2, origin], w_swapped.at[origin, k // HALVES], to_mate)

    def wide_all(origin, which, sem):
        ref = weights.at[pl.ds(0, 2), origin, which]
        return send(ref, ref, sem, sem, to_mate)

    def wide_from_mate(origin, w):
        ref = weights.at[w, origin, other]
        return send(ref, ref, w_send.at[2, origin], w_swapped.at[origin, w], to_mate)

    def share_wide(side):
        @pl.when(takes(side))
        def _():
            for k in range(WIDE):
                wide_side(side, wide_own(k), z, k).start()

    def x_to_hub(j):
        src, dst = ((ids_in, ids_peer), (x_in, x_peer))[j]
        return send(src, dst, t_send.at[j], t_recv.at[j], to_peer)

    @pl.when(client)
    def _():
        for j in range(2):
            x_to_hub(j).start()
        share_wide(1)
    share_wide(0)

    d_half = width // 2

    def down_own(i):
        cols = pl.ds(pl.multiple_of(i * d_half, d_half), d_half)
        return send(
            down_hbm.at[:, cols], weights.at[2, z, core, :, cols], d_send.at[0], d_recv.at[i], to_peer
        )

    def down_peer(i):
        cols = pl.ds(pl.multiple_of(i * d_half, d_half), d_half)
        here = weights.at[2, peer, core, :, cols]
        return send(here, here, d_swap.at[0], d_recv.at[i], to_mate)

    def down_own_mate():
        return send(down_hbm, weights.at[2, z, core], d_swap.at[0], d_swapped.at[0], to_mate)

    def down_peer_mate(i):
        cols = pl.ds(pl.multiple_of(i * d_half, d_half), d_half)
        here = weights.at[2, peer, core, :, cols]
        return send(here, here, d_swap.at[0], d_swapped.at[0], to_mate)

    def unit(q, which, cols=slice(None)):
        return weights.at[2, pl.ds(q * 2, 2), which, :, cols]

    def unit_side(side, q, cb):
        ref = unit(q, core, block(cb))
        return send(ref, ref, u_send.at[q], u_recv.at[q, cb], to_side(side))

    def unit_mate(q, cb):
        ref = unit(q, core, block(cb))
        return send(ref, ref, u_swap.at[q], u_swapped.at[q, cb], to_mate)

    def unit_from_mate(q, cb):
        ref = unit(q, other, block(cb))
        return send(ref, ref, u_swap.at[q], u_swapped.at[q, cb], to_mate)

    for i in range(2):
        down_own(i).start()

    @pl.when(hub)
    def _():
        for k in range(WIDE):
            wide_mate(wide_own(k), z, k).start()
    down_own_mate().start()

    local = [
        pltpu.make_async_copy(w, weights.at[k, z, core], local_sem.at[k])
        for k, w in enumerate((gate_hbm, up_hbm, down_hbm))
    ]
    my_rows = pl.ds(pl.multiple_of(me * tokens, tokens), tokens)
    local += [
        pltpu.make_async_copy(k_hbm, kv_buf.at[0, my_rows], local_sem.at[3]),
        pltpu.make_async_copy(v_hbm, kv_buf.at[1, my_rows], local_sem.at[4]),
        pltpu.make_async_copy(seg_in, seg_buf.at[me], local_sem.at[5]),
        pltpu.make_async_copy(q_hbm, q_buf, local_sem.at[6]),
    ]
    for copy in local:
        copy.start()

    t_row = lax.broadcasted_iota(jnp.int32, (tokens, tokens), 0)
    t_col = lax.broadcasted_iota(jnp.int32, (tokens, tokens), 1)

    def as_column(row):
        return jnp.sum(jnp.where(t_row == t_col, row, jnp.zeros_like(row)), axis=1, keepdims=True)

    def x_out(which, d):
        there = (mine + d) % n_exp
        return send(
            rows_out.at[which, there], rows_in.at[which, d], x_send.at[which], x_recv.at[which], {"exp": there}
        )

    def x_all(which):
        ref = rows_in.at[which, pl.ds(1, n_exp - 1)]
        return send(ref, ref, x_send.at[which], x_recv.at[which], to_mate)

    def route(which, ids_ref, x_ref):
        ids = ids_ref[...]
        row0, row1 = ids[0:1, :], ids[1:2, :]
        e_row = lax.broadcasted_iota(jnp.int32, (n_exp, tokens), 0)
        named_row = jnp.where((e_row == row0) | (e_row == row1), 1.0, 0.0).astype(F32)
        after = jnp.where(t_row < t_col, 1.0, 0.0).astype(BF16)
        rank_row = jnp.dot(named_row.astype(BF16), after, preferred_element_type=F32)
        place_row = lax.broadcasted_iota(jnp.int32, (cap, tokens), 0).astype(F32)
        x = x_ref[...]
        for e in range(n_exp):
            chosen = jnp.where(place_row == rank_row[e : e + 1, :], named_row[e : e + 1, :], 0.0)
            rows_out[which, e] = jnp.dot(chosen.astype(BF16), x, preferred_element_type=F32).astype(BF16)
        for d in range(1, n_exp):
            x_out(which, d).start()
        rows_in[which, 0] = rows_out[which, mine]

    @pl.when(hub)
    def _():
        route(1, ids_in, x_in)

    def kv_relay(s, carry):
        origin = z - s

        @pl.when(origin >= 0)
        def _():
            slot = origin * 2 + core
            for copy in kv_wait(slot, kv_recv.at[slot]):
                copy.wait_recv()

            @pl.when(has_side(1))
            def _():
                for copy in kv_copies(origin, kv_send, to_side(1)):
                    copy.start()

            for copy in kv_copies(origin, kv_swap, to_mate):
                copy.start()

        return carry

    lax.fori_loop(1, n_z, kv_relay, 0)

    @pl.when(hub)
    def _():
        share_wide(1)

    ids = ids_in[...]
    probs = prob_in[...]
    id0, id1 = as_column(ids[0:1, :]), as_column(ids[1:2, :])
    e_col = lax.broadcasted_iota(jnp.int32, (tokens, n_exp), 1)
    named_col = jnp.where((e_col == id0) | (e_col == id1), 1.0, 0.0).astype(F32)
    before = jnp.where(t_col < t_row, 1.0, 0.0).astype(BF16)
    rank_col = jnp.dot(before, named_col.astype(BF16), preferred_element_type=F32)
    weight_col = jnp.where(e_col == id0, as_column(probs[0:1, :]), 0.0) + jnp.where(
        e_col == id1, as_column(probs[1:2, :]), 0.0
    )
    place_col = lax.broadcasted_iota(jnp.int32, (tokens, cap), 1).astype(F32)
    for e in range(n_exp):
        back = jnp.where(place_col == rank_col[:, e : e + 1], named_col[:, e : e + 1], 0.0)
        pick[e] = back.astype(BF16)
        gates[e] = weight_col[:, e : e + 1]

    def kv_from_mate(origin, carry):
        @pl.when(origin <= z)
        def _():
            slot = origin * 2 + other
            for copy in kv_wait(slot, kv_recv.at[slot]):
                copy.wait_recv()

        @pl.when(origin > z)
        def _():
            both = pl.ds(pl.multiple_of(origin * 2 * tokens, 2 * tokens), 2 * tokens)
            kv_buf[:, both] = jnp.zeros((2, 2 * tokens, kv_buf.shape[2]), BF16)
            seg_buf[pl.ds(origin * 2, 2)] = jnp.zeros((2, 1, tokens), jnp.int32)

        return carry

    lax.fori_loop(0, n_z, kv_from_mate, 0)
    for copy in local[3:]:
        copy.wait()

    own_segment = jnp.sum(
        jnp.where(t_row == t_col, jnp.broadcast_to(seg_buf[me], (tokens, tokens)), 0), axis=1, keepdims=True
    )
    source_segment = jnp.where(own_segment % 2 == 1, own_segment - 1, own_segment)
    for c in range(n_ctx):
        theirs = seg_buf[c]
        allowed = (t_col + c * tokens <= t_row + me * tokens) & (
            (theirs == own_segment) | (theirs == source_segment)
        )
        bias[:, c * tokens : (c + 1) * tokens] = jnp.where(allowed, 0.0, -1e30)

    def relay_wide(s, k):
        for side in (0, 1):
            origin = z - s if side else z + s

            @pl.when((origin >= 0) & (origin < n_z) & inner)
            def _():
                here = wide_piece(k, origin)
                wide_side(side, here, origin, k).wait_recv()

                @pl.when(takes(side))
                def _():
                    wide_side(side, here, origin, k).start()

                @pl.when(hub)
                def _():
                    wide_mate(here, origin, k).start()

    scale = HEAD_SIZE ** -0.5 * math.log2(math.e)

    def attend(g, carry):
        lanes = pl.ds(pl.multiple_of(g * HEAD_SIZE, HEAD_SIZE), HEAD_SIZE)

        def heads(i, inner_carry):
            for u in range(HEADS_AT_ONCE):
                head = g * group + i * HEADS_AT_ONCE + u
                at = pl.ds(pl.multiple_of(head * HEAD_SIZE, HEAD_SIZE), HEAD_SIZE)
                scores = lax.dot_general(
                    q_buf[:, at], kv_buf[0, :, lanes], (((1,), (1,)), ((), ())), preferred_element_type=F32
                )
                scores = scores * scale + bias[...]
                peak = jnp.max(scores, axis=1, keepdims=True)
                power = jnp.exp2(scores - peak)
                share = 1.0 / jnp.sum(power, axis=1, keepdims=True)
                mixed = jnp.dot(power.astype(BF16), kv_buf[1, :, lanes], preferred_element_type=F32)
                q_buf[:, at] = (mixed * share).astype(BF16)
            return inner_carry

        lax.fori_loop(0, group // HEADS_AT_ONCE, heads, 0)

        @pl.when((g == 1) & hub)
        def _():
            for j in range(2):
                x_to_hub(j).wait_recv()
            route(0, ids_peer, x_peer)

        for k in range(WIDE):
            @pl.when(g == min(k + 1, KEY_HEAD_COUNT - 1))
            def _():
                relay_wide(1, k)

        return carry

    lax.fori_loop(0, KEY_HEAD_COUNT, attend, 0)
    ctx_copy = pltpu.make_async_copy(q_buf, ctx_out, out_sem.at[0])
    ctx_copy.start()

    @pl.when(hub)
    def _():
        for which in (1, 0):
            x_all(which).wait_recv()
    for copy in local[:3]:
        copy.wait()

    def h_back(origin):
        return send(hidden.at[0, origin], hidden.at[1, origin], h_send.at[0], h_recv.at[0], to_peer)

    h_all = send(hidden.at[0], hidden.at[1], h_send.at[0], h_recv.at[0], to_peer)

    def product(origin, w):
        wide_from_mate(origin, w).wait_recv()
        return lax.dot_general(
            rows_in[...].reshape(2 * n_exp * cap, width), weights[w, origin].reshape(-1, width),
            (((1,), (1,)), ((), ())), preferred_element_type=F32,
        )

    def gate_of(origin):
        gate = product(origin, 0)
        gated[...] = gate / (1.0 + jnp.exp(-gate))

    def hidden_of(origin):
        units = (gated[...] * product(origin, 1)).astype(BF16)
        hidden[0, origin] = units[: n_exp * cap]
        hidden[1, origin] = units[n_exp * cap :]
        h_back(origin).start()

    def pair_half(i):
        down_peer(i).wait_recv()
        per = COLUMN_BLOCKS // 2
        for side in (0, 1):
            @pl.when(has_side(side) & jnp.logical_not(peer_side(side)))
            def _():
                for c in range(per):
                    unit_side(side, pair, i * per + c).start()
        down_peer_mate(i).start()

    def each_other(what):
        def one(s, carry):
            for side in (0, 1):
                q = pair - s if side else pair + s

                @pl.when((q >= 0) & (q < n_pair))
                def _():
                    what(side, q)

            return carry

        lax.fori_loop(1, n_pair, one, 0)

    def pass_units(cb):
        def one(side, q):
            ref = unit(q, core, block(cb))
            send(ref, ref, u_send.at[q], u_recv.at[q, cb], to_mate).wait_recv()

            @pl.when(has_side(side))
            def _():
                unit_side(side, q, cb).start()

            unit_mate(q, cb).start()

        each_other(one)

    early = 3 if n_pair == 2 else 0
    ahead = hub & (z < n_z // 2) & (early > 0)

    def far(t, carry):
        s = (t + 1) // 2
        origin = z + jnp.where(t % 2 == 1, -toward, toward) * s

        @pl.when(t == 2)
        def _():
            pair_half(0)

        @pl.when(t == jnp.where(z < n_z // 2, 2 * n_z - 1, 3))
        def _():
            pair_half(1)

        here = hub & (origin >= 0) & (origin < n_z) & (t < 2 * n_z - 1)
        for w, what in enumerate((gate_of, hidden_of)):
            @pl.when(ahead & (t == 3))
            def _():
                pass_units(w)

            @pl.when((t % 2 == 1) & (s > 1))
            def _():
                for k in range(w * HALVES, (w + 1) * HALVES):
                    relay_wide(s, k)

            @pl.when(here)
            def _():
                what(origin)

        return carry

    lax.fori_loop(0, 2 * n_z, far, 0)

    @pl.when(ahead)
    def _():
        pass_units(2)

    @pl.when(jnp.logical_not(ahead))
    def _():
        pass_units(0)

    @pl.when(client)
    def _():
        h_all.wait_recv()
    hidden_all[...] = jnp.concatenate([hidden[1, o] for o in range(n_z)], axis=1)
    own_unit = unit(pair, other)
    send(own_unit, own_unit, d_swap.at[0], d_swapped.at[0], to_mate).wait_recv()

    def r_out(d, cb):
        return send(
            result.at[d, :, block(cb)], returned.at[d - 1, :, block(cb)],
            r_send.at[0], r_recv.at[cb], {"exp": (mine + n_exp - d) % n_exp},
        )

    def r_block(cb):
        ref = returned.at[:, :, block(cb)]
        return send(ref, ref, r_send.at[0], r_recv.at[cb], to_mate)

    def mix_copy(cb):
        return pltpu.make_async_copy(mix_buf.at[:, block(cb)], mix_out.at[:, block(cb)], out_sem.at[1])

    def combine(cb):
        at = block(cb)
        mix = gates[mine] * jnp.dot(pick[mine], result[0, :, at], preferred_element_type=F32)
        r_block(cb).wait_recv()
        for d in range(1, n_exp):
            source = (mine + d) % n_exp
            mix += gates[source] * jnp.dot(pick[source], returned[d - 1, :, at], preferred_element_type=F32)
        mix_buf[:, at] = mix.astype(BF16)
        mix_copy(cb).start()

    def early_sends():
        @pl.when(has_side(1))
        def _():
            for copy in kv_wait(me, kv_send.at[z]):
                copy.wait_send()
        for copy in kv_wait(me, kv_swap.at[z]):
            copy.wait_send()

        def kv_sent(s, carry):
            origin = z - s

            @pl.when(origin >= 0)
            def _():
                @pl.when(has_side(1))
                def _():
                    for copy in kv_wait(origin * 2 + core, kv_send.at[origin]):
                        copy.wait_send()

                for copy in kv_wait(origin * 2 + core, kv_swap.at[origin]):
                    copy.wait_send()

            return carry

        lax.fori_loop(1, n_z, kv_sent, 0)

        @pl.when(client)
        def _():
            for j in range(2):
                x_to_hub(j).wait_send()

        @pl.when(hub)
        def _():
            for which in (0, 1):
                x_all(which).wait_send()
            h_all.wait_send()

        def wide_sent(origin, carry):
            for side in (0, 1):
                @pl.when(takes(side) & ((origin == z) | (inner & (origin < z if side else origin > z))))
                def _():
                    wide_all(origin, core, w_send.at[side, origin]).wait_send()

            @pl.when(hub)
            def _():
                wide_all(origin, core, w_send.at[2, origin]).wait_send()

            return carry

        lax.fori_loop(0, n_z, wide_sent, 0)
        d_all = weights.at[2, z, core]
        send(d_all, d_all, d_send.at[0], d_recv.at[0], to_mate).wait_send()
        swapped = unit(pair, core)
        send(swapped, swapped, d_swap.at[0], d_swapped.at[0], to_mate).wait_send()

    def down_block(cb, carry):
        @pl.when(cb < COLUMN_BLOCKS)
        def _():
            each_other(lambda side, q: unit_from_mate(q, cb).wait_recv())
            down_w = weights[2, :, :, :, block(cb)].reshape(-1, columns)
            out = jnp.dot(hidden_all[...], down_w, preferred_element_type=F32)
            result[:, :, block(cb)] = out.astype(BF16).reshape(n_exp, cap, columns)
            for d in range(1, n_exp):
                r_out(d, cb).start()

        @pl.when((cb + 1 >= jnp.where(ahead, early, 1)) & (cb < COLUMN_BLOCKS - 1))
        def _():
            pass_units(cb + 1)

        @pl.when(cb >= LAG)
        def _():
            combine(cb - LAG)

        @pl.when(cb == LAG)
        def _():
            early_sends()

        return carry

    lax.fori_loop(0, COLUMN_BLOCKS + LAG, down_block, 0)

    for side in (0, 1):
        @pl.when(has_side(side) & jnp.logical_not(peer_side(side)))
        def _():
            ref = unit(pair, core)
            send(ref, ref, u_send.at[pair], u_send.at[pair], to_mate).wait_send()

    def units_sent(side, q):
        ref = unit(q, core)

        @pl.when(has_side(side))
        def _():
            send(ref, ref, u_send.at[q], u_send.at[q], to_mate).wait_send()

        send(ref, ref, u_swap.at[q], u_swap.at[q], to_mate).wait_send()

    each_other(units_sent)
    send(returned, returned, r_send.at[0], r_send.at[0], to_mate).wait_send()
    pltpu.make_async_copy(mix_buf, mix_out, out_sem.at[1]).wait()
    ctx_copy.wait()


def on_device(
    n_ctx, n_exp,
    queries, key_head_vectors, value_head_vectors, segment_ids,
    normed, expert_ids, gate_probs, gate_weight, up_weight, down_weight,
):
    tokens, q_width = queries.shape[1:]
    kv_width = key_head_vectors.shape[2]
    width = normed.shape[2]
    hidden = gate_weight.shape[1]
    most = tokens * expert_ids.shape[2] * 5 // (4 * n_exp)
    cap = -(-most // 16) * 16
    span = n_ctx * tokens
    n_z = n_ctx // 2
    dma = pltpu.SemaphoreType.DMA
    hbm = pl.BlockSpec(memory_space=pl.ANY)
    vmem = pl.BlockSpec(memory_space=pltpu.VMEM)
    context, mixture = pl.pallas_call(
        functools.partial(kernel, n_ctx, n_exp, cap),
        out_shape=(
            jax.ShapeDtypeStruct((tokens, q_width), BF16),
            jax.ShapeDtypeStruct((tokens, width), BF16),
        ),
        in_specs=[hbm, hbm, hbm, vmem, vmem, vmem, vmem, hbm, hbm, hbm],
        out_specs=(hbm, hbm),
        scratch_shapes=[
            pltpu.VMEM((tokens, q_width), BF16),
            pltpu.VMEM((2, span, kv_width), BF16),
            pltpu.VMEM((n_ctx, 1, tokens), jnp.int32),
            pltpu.VMEM((tokens, span), F32),
            pltpu.VMEM((3, n_z, 2, hidden, width), BF16),
            pltpu.VMEM((tokens, width), BF16),
            pltpu.VMEM((expert_ids.shape[2], tokens), jnp.int32),
            pltpu.VMEM((2, n_exp, cap, width), BF16),
            pltpu.VMEM((2, n_exp, cap, width), BF16),
            pltpu.VMEM((2, n_z, n_exp * cap, 2 * hidden), BF16),
            pltpu.VMEM((2 * n_exp * cap, 2 * hidden), F32),
            pltpu.VMEM((n_exp * cap, n_ctx * hidden), BF16),
            pltpu.VMEM((n_exp, cap, width), BF16),
            pltpu.VMEM((n_exp - 1, cap, width), BF16),
            pltpu.VMEM((n_exp, tokens, cap), BF16),
            pltpu.VMEM((n_exp, tokens, 1), F32),
            pltpu.VMEM((tokens, width), BF16),
            dma((7,)),
            dma((n_z, 2)),
            dma((n_z, 2)),
            dma((n_ctx, 2)),
            dma((3, n_z)),
            dma((n_z, WIDE)),
            dma((n_z, 2)),
            dma((1,)),
            dma((2,)),
            dma((1,)),
            dma((1,)),
            dma((n_z // 2,)),
            dma((n_z // 2, COLUMN_BLOCKS)),
            dma((n_z // 2,)),
            dma((n_z // 2, COLUMN_BLOCKS)),
            dma((2,)),
            dma((2,)),
            dma((2,)),
            dma((2,)),
            dma((1,)),
            dma((1,)),
            dma((1,)),
            dma((COLUMN_BLOCKS,)),
            dma((2,)),
        ],
        compiler_params=pltpu.CompilerParams(
            collective_id=0, has_side_effects=True, vmem_limit_bytes=60 * 1024 * 1024
        ),
        name="layer",
    )(
        queries[0], key_head_vectors[0], value_head_vectors[0], segment_ids,
        normed[0], expert_ids[0].T, gate_probs[0].T, gate_weight[0], up_weight[0], down_weight[0],
    )
    return context[None], mixture[None]


def solution(mesh):
    rows = P("exp", "ctx", None)
    in_specs = (rows, rows, rows, P("exp", "ctx"), rows, rows, rows, rows, rows, rows)
    return jax.shard_map(
        functools.partial(on_device, mesh.shape["ctx"], mesh.shape["exp"]),
        mesh=mesh, in_specs=in_specs, out_specs=(rows, rows), check_vma=False,
    )
```

```python
import functools
import math

import jax
import jax.numpy as jnp
from jax import lax
from jax.experimental import pallas as pl
from jax.experimental.pallas import tpu as pltpu
from jax.sharding import PartitionSpec as P

KEY_HEAD_COUNT = 4
HEAD_SIZE = 128
COLUMN_BLOCKS = 16
HEADS_AT_ONCE = 4
HALVES = 2
WIDE = 2 * HALVES
LAG = 2
MESH = pl.DeviceIdType.MESH
F32 = jnp.float32
BF16 = jnp.bfloat16


def kernel(
    n_ctx, n_exp, cap,
    q_hbm, k_hbm, v_hbm, seg_in, x_in, ids_in, prob_in, gate_hbm, up_hbm, down_hbm,
    ctx_out, mix_out,
    q_buf, kv_buf, seg_buf, bias, weights, x_peer, ids_peer, rows_out, rows_in,
    hidden, gated, hidden_all, result, returned, pick, gates, mix_buf,
    local_sem, kv_send, kv_swap, kv_recv, w_send, w_recv, w_swapped,
    d_send, d_recv, d_swap, d_swapped, u_send, u_recv, u_swap, u_swapped,
    t_send, t_recv, x_send, x_recv, h_send, h_recv, r_send, r_recv, out_sem,
):
    me = lax.axis_index("ctx")
    mine = lax.axis_index("exp")
    n_z = n_ctx // 2
    n_pair = n_z // 2
    z, core = me // 2, me % 2
    other = 1 - core
    mate = me + 1 - 2 * core
    toward = 1 - 2 * (z % 2)
    peer = z + toward
    pair = z // 2
    hub = jnp.where(z < n_z // 2, z % 2 == 1, z % 2 == 0)
    client = jnp.logical_not(hub)
    inner = (z > 0) & (z < n_z - 1)
    tokens, width = x_in.shape
    group = q_buf.shape[1] // (KEY_HEAD_COUNT * HEAD_SIZE)
    columns = width // COLUMN_BLOCKS
    half = width // HALVES

    def send(src, dst, send_sem, recv_sem, where):
        return pltpu.make_async_remote_copy(
            src_ref=src, dst_ref=dst, send_sem=send_sem, recv_sem=recv_sem,
            device_id=where, device_id_type=MESH,
        )

    to_mate = {"ctx": mate}
    to_peer = {"ctx": peer * 2 + core}

    def to_side(side):
        return {"ctx": me + 2 if side else me - 2}

    def block(cb):
        return pl.ds(pl.multiple_of(cb * columns, columns), columns)

    def has_side(side):
        return z + 1 < n_z if side else z > 0

    def takes(side):
        return z + 1 < n_z - 1 if side else z > 1

    def peer_side(side):
        return z % 2 == 1 - side

    barrier = pltpu.get_barrier_semaphore()
    for side in (0, 1):
        @pl.when(has_side(side))
        def _():
            pl.semaphore_signal(barrier, inc=1, device_id=to_side(side), device_id_type=MESH)
    pl.semaphore_signal(barrier, inc=1, device_id=to_mate, device_id_type=MESH)
    for d in range(1, n_exp):
        pl.semaphore_signal(barrier, inc=1, device_id={"exp": (mine + d) % n_exp}, device_id_type=MESH)
    pl.semaphore_wait(barrier, n_exp + jnp.where(inner, 2, 1))

    def kv_rows(slot):
        return kv_buf.at[:, pl.ds(pl.multiple_of(slot * tokens, tokens), tokens)]

    def kv_copies(origin, sem, where, own=False):
        slot = origin * 2 + core
        rows = pl.ds(pl.multiple_of(slot * tokens, tokens), tokens)
        if own:
            pairs = [(k_hbm, kv_buf.at[0, rows], 0), (v_hbm, kv_buf.at[1, rows], 0), (seg_in, seg_buf.at[slot], 1)]
        else:
            pairs = [(kv_rows(slot), kv_rows(slot), 0), (seg_buf.at[slot], seg_buf.at[slot], 1)]
        return [send(src, dst, sem.at[origin, j], kv_recv.at[slot, j], where) for src, dst, j in pairs]

    def kv_wait(slot, sems):
        refs = (kv_rows(slot), seg_buf.at[slot])
        return [send(refs[j], refs[j], sems.at[j], sems.at[j], to_mate) for j in range(2)]

    @pl.when(has_side(1))
    def _():
        for copy in kv_copies(z, kv_send, to_side(1), own=True):
            copy.start()
    for copy in kv_copies(z, kv_swap, to_mate, own=True):
        copy.start()

    def wide_own(k):
        return (gate_hbm, up_hbm)[k // HALVES].at[:, pl.ds(k % HALVES * half, half)]

    def wide_piece(k, origin):
        return weights.at[k // HALVES, origin, core, :, pl.ds(k % HALVES * half, half)]

    def wide_side(side, src, origin, k):
        return send(src, wide_piece(k, origin), w_send.at[side, origin], w_recv.at[origin, k], to_side(side))

    def wide_mate(src, origin, k):
        return send(src, wide_piece(k, origin), w_send.at[2, origin], w_swapped.at[origin, k // HALVES], to_mate)

    def wide_all(origin, which, sem):
        ref = weights.at[pl.ds(0, 2), origin, which]
        return send(ref, ref, sem, sem, to_mate)

    def wide_from_mate(origin, w):
        ref = weights.at[w, origin, other]
        return send(ref, ref, w_send.at[2, origin], w_swapped.at[origin, w], to_mate)

    def share_wide(side):
        @pl.when(takes(side))
        def _():
            for k in range(WIDE):
                wide_side(side, wide_own(k), z, k).start()

    def x_to_hub(j):
        src, dst = ((ids_in, ids_peer), (x_in, x_peer))[j]
        return send(src, dst, t_send.at[j], t_recv.at[j], to_peer)

    @pl.when(client)
    def _():
        for j in range(2):
            x_to_hub(j).start()
        share_wide(1)
    share_wide(0)

    d_half = width // 2

    def down_own(i):
        cols = pl.ds(pl.multiple_of(i * d_half, d_half), d_half)
        return send(
            down_hbm.at[:, cols], weights.at[2, z, core, :, cols], d_send.at[0], d_recv.at[i], to_peer
        )

    def down_peer(i):
        cols = pl.ds(pl.multiple_of(i * d_half, d_half), d_half)
        here = weights.at[2, peer, core, :, cols]
        return send(here, here, d_swap.at[0], d_recv.at[i], to_mate)

    def down_own_mate():
        return send(down_hbm, weights.at[2, z, core], d_swap.at[0], d_swapped.at[0], to_mate)

    def down_peer_mate(i):
        cols = pl.ds(pl.multiple_of(i * d_half, d_half), d_half)
        here = weights.at[2, peer, core, :, cols]
        return send(here, here, d_swap.at[0], d_swapped.at[0], to_mate)

    def unit(q, which, cols=slice(None)):
        return weights.at[2, pl.ds(q * 2, 2), which, :, cols]

    def unit_side(side, q, cb):
        ref = unit(q, core, block(cb))
        return send(ref, ref, u_send.at[q], u_recv.at[q, cb], to_side(side))

    def unit_mate(q, cb):
        ref = unit(q, core, block(cb))
        return send(ref, ref, u_swap.at[q], u_swapped.at[q, cb], to_mate)

    def unit_from_mate(q, cb):
        ref = unit(q, other, block(cb))
        return send(ref, ref, u_swap.at[q], u_swapped.at[q, cb], to_mate)

    for i in range(2):
        down_own(i).start()

    @pl.when(hub)
    def _():
        for k in range(WIDE):
            wide_mate(wide_own(k), z, k).start()
    down_own_mate().start()

    local = [
        pltpu.make_async_copy(w, weights.at[k, z, core], local_sem.at[k])
        for k, w in enumerate((gate_hbm, up_hbm, down_hbm))
    ]
    my_rows = pl.ds(pl.multiple_of(me * tokens, tokens), tokens)
    local += [
        pltpu.make_async_copy(k_hbm, kv_buf.at[0, my_rows], local_sem.at[3]),
        pltpu.make_async_copy(v_hbm, kv_buf.at[1, my_rows], local_sem.at[4]),
        pltpu.make_async_copy(seg_in, seg_buf.at[me], local_sem.at[5]),
        pltpu.make_async_copy(q_hbm, q_buf, local_sem.at[6]),
    ]
    for copy in local:
        copy.start()

    t_row = lax.broadcasted_iota(jnp.int32, (tokens, tokens), 0)
    t_col = lax.broadcasted_iota(jnp.int32, (tokens, tokens), 1)

    def as_column(row):
        return jnp.sum(jnp.where(t_row == t_col, row, jnp.zeros_like(row)), axis=1, keepdims=True)

    def x_out(which, d):
        there = (mine + d) % n_exp
        return send(
            rows_out.at[which, there], rows_in.at[which, d], x_send.at[which], x_recv.at[which], {"exp": there}
        )

    def x_all(which):
        ref = rows_in.at[which, pl.ds(1, n_exp - 1)]
        return send(ref, ref, x_send.at[which], x_recv.at[which], to_mate)

    def route(which, ids_ref, x_ref):
        ids = ids_ref[...]
        row0, row1 = ids[0:1, :], ids[1:2, :]
        e_row = lax.broadcasted_iota(jnp.int32, (n_exp, tokens), 0)
        named_row = jnp.where((e_row == row0) | (e_row == row1), 1.0, 0.0).astype(F32)
        after = jnp.where(t_row < t_col, 1.0, 0.0).astype(BF16)
        rank_row = jnp.dot(named_row.astype(BF16), after, preferred_element_type=F32)
        place_row = lax.broadcasted_iota(jnp.int32, (cap, tokens), 0).astype(F32)
        x = x_ref[...]
        for e in range(n_exp):
            chosen = jnp.where(place_row == rank_row[e : e + 1, :], named_row[e : e + 1, :], 0.0)
            rows_out[which, e] = jnp.dot(chosen.astype(BF16), x, preferred_element_type=F32).astype(BF16)
        for d in range(1, n_exp):
            x_out(which, d).start()
        rows_in[which, 0] = rows_out[which, mine]

    @pl.when(hub)
    def _():
        route(1, ids_in, x_in)

    def kv_relay(s, carry):
        origin = z - s

        @pl.when(origin >= 0)
        def _():
            slot = origin * 2 + core
            for copy in kv_wait(slot, kv_recv.at[slot]):
                copy.wait_recv()

            @pl.when(has_side(1))
            def _():
                for copy in kv_copies(origin, kv_send, to_side(1)):
                    copy.start()

            for copy in kv_copies(origin, kv_swap, to_mate):
                copy.start()

        return carry

    lax.fori_loop(1, n_z, kv_relay, 0)

    @pl.when(hub)
    def _():
        share_wide(1)

    ids = ids_in[...]
    probs = prob_in[...]
    id0, id1 = as_column(ids[0:1, :]), as_column(ids[1:2, :])
    e_col = lax.broadcasted_iota(jnp.int32, (tokens, n_exp), 1)
    named_col = jnp.where((e_col == id0) | (e_col == id1), 1.0, 0.0).astype(F32)
    before = jnp.where(t_col < t_row, 1.0, 0.0).astype(BF16)
    rank_col = jnp.dot(before, named_col.astype(BF16), preferred_element_type=F32)
    weight_col = jnp.where(e_col == id0, as_column(probs[0:1, :]), 0.0) + jnp.where(
        e_col == id1, as_column(probs[1:2, :]), 0.0
    )
    place_col = lax.broadcasted_iota(jnp.int32, (tokens, cap), 1).astype(F32)
    for e in range(n_exp):
        back = jnp.where(place_col == rank_col[:, e : e + 1], named_col[:, e : e + 1], 0.0)
        pick[e] = back.astype(BF16)
        gates[e] = weight_col[:, e : e + 1]

    def kv_from_mate(origin, carry):
        @pl.when(origin <= z)
        def _():
            slot = origin * 2 + other
            for copy in kv_wait(slot, kv_recv.at[slot]):
                copy.wait_recv()

        @pl.when(origin > z)
        def _():
            both = pl.ds(pl.multiple_of(origin * 2 * tokens, 2 * tokens), 2 * tokens)
            kv_buf[:, both] = jnp.zeros((2, 2 * tokens, kv_buf.shape[2]), BF16)
            seg_buf[pl.ds(origin * 2, 2)] = jnp.zeros((2, 1, tokens), jnp.int32)

        return carry

    lax.fori_loop(0, n_z, kv_from_mate, 0)
    for copy in local[3:]:
        copy.wait()

    own_segment = jnp.sum(
        jnp.where(t_row == t_col, jnp.broadcast_to(seg_buf[me], (tokens, tokens)), 0), axis=1, keepdims=True
    )
    source_segment = jnp.where(own_segment % 2 == 1, own_segment - 1, own_segment)
    for c in range(n_ctx):
        theirs = seg_buf[c]
        allowed = (t_col + c * tokens <= t_row + me * tokens) & (
            (theirs == own_segment) | (theirs == source_segment)
        )
        bias[:, c * tokens : (c + 1) * tokens] = jnp.where(allowed, 0.0, -1e30)

    def relay_wide(s, k):
        for side in (0, 1):
            origin = z - s if side else z + s

            @pl.when((origin >= 0) & (origin < n_z) & inner)
            def _():
                here = wide_piece(k, origin)
                wide_side(side, here, origin, k).wait_recv()

                @pl.when(takes(side))
                def _():
                    wide_side(side, here, origin, k).start()

                @pl.when(hub)
                def _():
                    wide_mate(here, origin, k).start()

    scale = HEAD_SIZE ** -0.5 * math.log2(math.e)

    def attend(g, carry):
        lanes = pl.ds(pl.multiple_of(g * HEAD_SIZE, HEAD_SIZE), HEAD_SIZE)

        def heads(i, inner_carry):
            for u in range(HEADS_AT_ONCE):
                head = g * group + i * HEADS_AT_ONCE + u
                at = pl.ds(pl.multiple_of(head * HEAD_SIZE, HEAD_SIZE), HEAD_SIZE)
                scores = lax.dot_general(
                    q_buf[:, at], kv_buf[0, :, lanes], (((1,), (1,)), ((), ())), preferred_element_type=F32
                )
                scores = scores * scale + bias[...]
                peak = jnp.max(scores, axis=1, keepdims=True)
                power = jnp.exp2(scores - peak)
                share = 1.0 / jnp.sum(power, axis=1, keepdims=True)
                mixed = jnp.dot(power.astype(BF16), kv_buf[1, :, lanes], preferred_element_type=F32)
                q_buf[:, at] = (mixed * share).astype(BF16)
            return inner_carry

        lax.fori_loop(0, group // HEADS_AT_ONCE, heads, 0)

        @pl.when((g == 1) & hub)
        def _():
            for j in range(2):
                x_to_hub(j).wait_recv()
            route(0, ids_peer, x_peer)

        for k in range(WIDE):
            @pl.when(g == min(k + 1, KEY_HEAD_COUNT - 1))
            def _():
                relay_wide(1, k)

        return carry

    lax.fori_loop(0, KEY_HEAD_COUNT, attend, 0)
    ctx_copy = pltpu.make_async_copy(q_buf, ctx_out, out_sem.at[0])
    ctx_copy.start()

    @pl.when(hub)
    def _():
        for which in (1, 0):
            x_all(which).wait_recv()
    for copy in local[:3]:
        copy.wait()

    def h_back(origin):
        return send(hidden.at[0, origin], hidden.at[1, origin], h_send.at[0], h_recv.at[0], to_peer)

    h_all = send(hidden.at[0], hidden.at[1], h_send.at[0], h_recv.at[0], to_peer)

    def product(origin, w, which):
        return lax.dot_general(
            rows_in[which].reshape(-1, width), weights[w, origin].reshape(-1, width),
            (((1,), (1,)), ((), ())), preferred_element_type=F32,
        )

    def gate_of(origin):
        wide_from_mate(origin, 0).wait_recv()
        gate = product(origin, 0, slice(None))
        gated[...] = gate / (1.0 + jnp.exp(-gate))

    def hidden_of(origin):
        wide_from_mate(origin, 1).wait_recv()
        rows = n_exp * cap
        hidden[0, origin] = (gated[:rows] * product(origin, 1, 0)).astype(BF16)
        h_back(origin).start()
        hidden[1, origin] = (gated[rows:] * product(origin, 1, 1)).astype(BF16)

    def pair_half(i):
        down_peer(i).wait_recv()
        per = COLUMN_BLOCKS // 2
        for side in (0, 1):
            @pl.when(has_side(side) & jnp.logical_not(peer_side(side)))
            def _():
                for c in range(per):
                    unit_side(side, pair, i * per + c).start()
        down_peer_mate(i).start()

    def each_other(what):
        def one(s, carry):
            for side in (0, 1):
                q = pair - s if side else pair + s

                @pl.when((q >= 0) & (q < n_pair))
                def _():
                    what(side, q)

            return carry

        lax.fori_loop(1, n_pair, one, 0)

    def pass_units(cb):
        def one(side, q):
            ref = unit(q, core, block(cb))
            send(ref, ref, u_send.at[q], u_recv.at[q, cb], to_mate).wait_recv()

            @pl.when(has_side(side))
            def _():
                unit_side(side, q, cb).start()

            unit_mate(q, cb).start()

        each_other(one)

    early = 3 if n_pair == 2 else 0
    ahead = hub & (z < n_z // 2) & (early > 0)

    def far(t, carry):
        s = (t + 1) // 2
        origin = z + jnp.where(t % 2 == 1, -toward, toward) * s

        @pl.when(t == 2)
        def _():
            pair_half(0)

        @pl.when(t == jnp.where(z < n_z // 2, 2 * n_z - 1, 3))
        def _():
            pair_half(1)

        here = hub & (origin >= 0) & (origin < n_z) & (t < 2 * n_z - 1)
        for w, what in enumerate((gate_of, hidden_of)):
            @pl.when(ahead & (t == 3))
            def _():
                pass_units(w)

            @pl.when((t % 2 == 1) & (s > 1))
            def _():
                for k in range(w * HALVES, (w + 1) * HALVES):
                    relay_wide(s, k)

            @pl.when(here)
            def _():
                what(origin)

        return carry

    lax.fori_loop(0, 2 * n_z, far, 0)

    @pl.when(ahead)
    def _():
        pass_units(2)

    @pl.when(jnp.logical_not(ahead))
    def _():
        pass_units(0)

    @pl.when(client)
    def _():
        h_all.wait_recv()
    hidden_all[...] = jnp.concatenate([hidden[1, o] for o in range(n_z)], axis=1)
    own_unit = unit(pair, other)
    send(own_unit, own_unit, d_swap.at[0], d_swapped.at[0], to_mate).wait_recv()

    def r_out(d, cb):
        return send(
            result.at[d, :, block(cb)], returned.at[d - 1, :, block(cb)],
            r_send.at[0], r_recv.at[cb], {"exp": (mine + n_exp - d) % n_exp},
        )

    def r_block(cb):
        ref = returned.at[:, :, block(cb)]
        return send(ref, ref, r_send.at[0], r_recv.at[cb], to_mate)

    def mix_copy(cb):
        return pltpu.make_async_copy(mix_buf.at[:, block(cb)], mix_out.at[:, block(cb)], out_sem.at[1])

    def combine(cb):
        at = block(cb)
        mix = gates[mine] * jnp.dot(pick[mine], result[0, :, at], preferred_element_type=F32)
        r_block(cb).wait_recv()
        for d in range(1, n_exp):
            source = (mine + d) % n_exp
            mix += gates[source] * jnp.dot(pick[source], returned[d - 1, :, at], preferred_element_type=F32)
        mix_buf[:, at] = mix.astype(BF16)
        mix_copy(cb).start()

    def early_sends():
        @pl.when(has_side(1))
        def _():
            for copy in kv_wait(me, kv_send.at[z]):
                copy.wait_send()
        for copy in kv_wait(me, kv_swap.at[z]):
            copy.wait_send()

        def kv_sent(s, carry):
            origin = z - s

            @pl.when(origin >= 0)
            def _():
                @pl.when(has_side(1))
                def _():
                    for copy in kv_wait(origin * 2 + core, kv_send.at[origin]):
                        copy.wait_send()

                for copy in kv_wait(origin * 2 + core, kv_swap.at[origin]):
                    copy.wait_send()

            return carry

        lax.fori_loop(1, n_z, kv_sent, 0)

        @pl.when(client)
        def _():
            for j in range(2):
                x_to_hub(j).wait_send()

        @pl.when(hub)
        def _():
            for which in (0, 1):
                x_all(which).wait_send()
            h_all.wait_send()

        def wide_sent(origin, carry):
            for side in (0, 1):
                @pl.when(takes(side) & ((origin == z) | (inner & (origin < z if side else origin > z))))
                def _():
                    wide_all(origin, core, w_send.at[side, origin]).wait_send()

            @pl.when(hub)
            def _():
                wide_all(origin, core, w_send.at[2, origin]).wait_send()

            return carry

        lax.fori_loop(0, n_z, wide_sent, 0)
        d_all = weights.at[2, z, core]
        send(d_all, d_all, d_send.at[0], d_recv.at[0], to_mate).wait_send()
        swapped = unit(pair, core)
        send(swapped, swapped, d_swap.at[0], d_swapped.at[0], to_mate).wait_send()

    def down_block(cb, carry):
        @pl.when(cb < COLUMN_BLOCKS)
        def _():
            each_other(lambda side, q: unit_from_mate(q, cb).wait_recv())
            down_w = weights[2, :, :, :, block(cb)].reshape(-1, columns)
            out = jnp.dot(hidden_all[...], down_w, preferred_element_type=F32)
            result[:, :, block(cb)] = out.astype(BF16).reshape(n_exp, cap, columns)
            for d in range(1, n_exp):
                r_out(d, cb).start()

        @pl.when((cb + 1 >= jnp.where(ahead, early, 1)) & (cb < COLUMN_BLOCKS - 1))
        def _():
            pass_units(cb + 1)

        @pl.when(cb >= LAG)
        def _():
            combine(cb - LAG)

        @pl.when(cb == LAG)
        def _():
            early_sends()

        return carry

    lax.fori_loop(0, COLUMN_BLOCKS + LAG, down_block, 0)

    for side in (0, 1):
        @pl.when(has_side(side) & jnp.logical_not(peer_side(side)))
        def _():
            ref = unit(pair, core)
            send(ref, ref, u_send.at[pair], u_send.at[pair], to_mate).wait_send()

    def units_sent(side, q):
        ref = unit(q, core)

        @pl.when(has_side(side))
        def _():
            send(ref, ref, u_send.at[q], u_send.at[q], to_mate).wait_send()

        send(ref, ref, u_swap.at[q], u_swap.at[q], to_mate).wait_send()

    each_other(units_sent)
    send(returned, returned, r_send.at[0], r_send.at[0], to_mate).wait_send()
    pltpu.make_async_copy(mix_buf, mix_out, out_sem.at[1]).wait()
    ctx_copy.wait()


def on_device(
    n_ctx, n_exp,
    queries, key_head_vectors, value_head_vectors, segment_ids,
    normed, expert_ids, gate_probs, gate_weight, up_weight, down_weight,
):
    tokens, q_width = queries.shape[1:]
    kv_width = key_head_vectors.shape[2]
    width = normed.shape[2]
    hidden = gate_weight.shape[1]
    most = tokens * expert_ids.shape[2] * 5 // (4 * n_exp)
    cap = -(-most // 16) * 16
    span = n_ctx * tokens
    n_z = n_ctx // 2
    dma = pltpu.SemaphoreType.DMA
    hbm = pl.BlockSpec(memory_space=pl.ANY)
    vmem = pl.BlockSpec(memory_space=pltpu.VMEM)
    context, mixture = pl.pallas_call(
        functools.partial(kernel, n_ctx, n_exp, cap),
        out_shape=(
            jax.ShapeDtypeStruct((tokens, q_width), BF16),
            jax.ShapeDtypeStruct((tokens, width), BF16),
        ),
        in_specs=[hbm, hbm, hbm, vmem, vmem, vmem, vmem, hbm, hbm, hbm],
        out_specs=(hbm, hbm),
        scratch_shapes=[
            pltpu.VMEM((tokens, q_width), BF16),
            pltpu.VMEM((2, span, kv_width), BF16),
            pltpu.VMEM((n_ctx, 1, tokens), jnp.int32),
            pltpu.VMEM((tokens, span), F32),
            pltpu.VMEM((3, n_z, 2, hidden, width), BF16),
            pltpu.VMEM((tokens, width), BF16),
            pltpu.VMEM((expert_ids.shape[2], tokens), jnp.int32),
            pltpu.VMEM((2, n_exp, cap, width), BF16),
            pltpu.VMEM((2, n_exp, cap, width), BF16),
            pltpu.VMEM((2, n_z, n_exp * cap, 2 * hidden), BF16),
            pltpu.VMEM((2 * n_exp * cap, 2 * hidden), F32),
            pltpu.VMEM((n_exp * cap, n_ctx * hidden), BF16),
            pltpu.VMEM((n_exp, cap, width), BF16),
            pltpu.VMEM((n_exp - 1, cap, width), BF16),
            pltpu.VMEM((n_exp, tokens, cap), BF16),
            pltpu.VMEM((n_exp, tokens, 1), F32),
            pltpu.VMEM((tokens, width), BF16),
            dma((7,)),
            dma((n_z, 2)),
            dma((n_z, 2)),
            dma((n_ctx, 2)),
            dma((3, n_z)),
            dma((n_z, WIDE)),
            dma((n_z, 2)),
            dma((1,)),
            dma((2,)),
            dma((1,)),
            dma((1,)),
            dma((n_z // 2,)),
            dma((n_z // 2, COLUMN_BLOCKS)),
            dma((n_z // 2,)),
            dma((n_z // 2, COLUMN_BLOCKS)),
            dma((2,)),
            dma((2,)),
            dma((2,)),
            dma((2,)),
            dma((1,)),
            dma((1,)),
            dma((1,)),
            dma((COLUMN_BLOCKS,)),
            dma((2,)),
        ],
        compiler_params=pltpu.CompilerParams(
            collective_id=0, has_side_effects=True, vmem_limit_bytes=60 * 1024 * 1024
        ),
        name="layer",
    )(
        queries[0], key_head_vectors[0], value_head_vectors[0], segment_ids,
        normed[0], expert_ids[0].T, gate_probs[0].T, gate_weight[0], up_weight[0], down_weight[0],
    )
    return context[None], mixture[None]


def solution(mesh):
    rows = P("exp", "ctx", None)
    in_specs = (rows, rows, rows, P("exp", "ctx"), rows, rows, rows, rows, rows, rows)
    return jax.shard_map(
        functools.partial(on_device, mesh.shape["ctx"], mesh.shape["exp"]),
        mesh=mesh, in_specs=in_specs, out_specs=(rows, rows), check_vma=False,
    )
```
